32 devices in a mesh: grp: 2 (over y), ctx: 4 (over x, core), head: 4 (over z).
Axes of the slice: x: 2, y: 2, z: 4, core: 2. Of those that a mesh axis runs over, the one named last changes fastest.
Arguments:
- prompt_hidden: bfloat16 [4, 1024, 4096], P('grp', 'ctx', 'head'), parts along dimension 0, may hold values from -3 to 3
- qkv_weight: bfloat16 [3, 4096, 4096], P(None, 'ctx', 'head'), may hold values from -0.09375 to 0.09375
- out_weight: bfloat16 [4096, 4096], P('head', 'ctx'), may hold values from -0.9375 to 0.9375
- embed_table: bfloat16 [32768, 4096], P('ctx', 'head'), may hold values from -60 to 60
- response_ids: int32 [4, 256], P(None, 'grp'), parts along dimension 1, may hold values from 0 to 32767
- assignment: int32 [256], P('grp'), parts along dimension 0, may hold values from 0 to 1
Outputs:
- final_hidden: bfloat16 [4, 256, 4096], P(None, ('grp', 'ctx'), 'head'), parts along dimension 1
The draws below stay inside these ranges and needn't reach their ends.
There are 2 independent parts, one for each index of `grp`. The reference program is written for one: setup_inputs(seed, part) draws one part's arguments, and reference() takes and returns one part's arrays. A program takes and returns all parts, laid end to end along the dimension named above; an argument that names none is the same for every part. Nothing has to cross between parts.
All inputs are finite; a program needn't handle non-finite values.
Results may differ from the reference program's by a relative error of at most 0.023.
Values may be sent and summed in bfloat16 or wider, within the bound.
A program may use at most 128 MiB of HBM per device.

```python
import jax
import jax.numpy as jnp
from jax import lax

D = 4096
H = 32
VOCAB = 32768
DH = 128
STEPS = 4
PLEN = 1024
RESP = 128


def column_scale(key, width):
    position = jnp.arange(width, dtype=jnp.float32) / (width - 1)
    return (3.0 ** position)[None, :]


def draw_embed_table(key, part):
    base = jnp.clip(jax.random.normal(jax.random.fold_in(key, 3), (VOCAB, D), jnp.float32), -4.0, 4.0)
    return (base * column_scale(jax.random.fold_in(key, 5), D)).astype(jnp.bfloat16)


def draw_out_weight(key, part):
    base = jnp.clip(jax.random.normal(jax.random.fold_in(key, 11), (D, D), jnp.float32), -4.0, 4.0)
    scaled = base * column_scale(jax.random.fold_in(key, 13), D) / jnp.sqrt(jnp.float32(D))
    return jnp.clip(scaled, -0.9375, 0.9375).astype(jnp.bfloat16)


def set_ends(array, rng, low, top_value):
    extent = array.shape
    place = [jax.random.randint(jax.random.fold_in(rng, axis), (), 0, extent[axis]) for axis in range(len(extent))]
    array = array.at[tuple(place)].set(low)
    longest = extent.index(max(extent))
    place[longest] = (place[longest] + 1) % extent[longest]
    return array.at[tuple(place)].set(top_value)


def levels(own_key, shape, split, least, high):
    factor_of, own = 1.0, jax.random.fold_in(own_key, 6)
    for dim, blocks in split:
        heights = jnp.exp(jax.random.uniform(jax.random.fold_in(own, dim), (blocks,), jnp.float32, least / len(split), high / len(split)))
        factor_of = factor_of * jnp.repeat(heights, shape[dim] // blocks).reshape([-1 if axis == dim else 1 for axis in range(len(shape))])
    return factor_of


def scatter_about(own_key, dims, spread, reach, pieces=(), kind=jnp.bfloat16):
    loudness = levels(own_key, dims, pieces, -0.22, 0.18) if pieces else 1.0
    drawn = jax.random.normal(own_key, dims, jnp.float32) * spread * loudness
    return jnp.minimum(jnp.maximum(drawn, -reach), reach).astype(kind)


def setup_inputs(seed: int = 0, part: int = 0) -> dict:
    arg_keys = jax.random.split(jax.random.key(seed), 7)
    part_splits = jax.random.split(jax.random.fold_in(arg_keys[6], part), 7)
    prompt_hidden = scatter_about(part_splits[0], (2, PLEN, D), 0.5, 3.0, ((1, 4), (2, 4)))
    qkv_weight = scatter_about(arg_keys[1], (3, D, D), D ** -0.5, 0.09375, ((1, 4), (2, 4)))
    out_weight = draw_out_weight(jax.random.fold_in(arg_keys[6], 71), part)
    embed_table = draw_embed_table(jax.random.fold_in(arg_keys[6], 71), part)
    response_ids = set_ends(jax.random.randint(part_splits[4], (STEPS, RESP), 0, VOCAB), jax.random.fold_in(part_splits[4], 1), 0, VOCAB - 1).astype(jnp.int32)
    assignment = set_ends(jax.random.randint(part_splits[5], (RESP,), 0, 2), jax.random.fold_in(part_splits[5], 1), 0, 1).astype(jnp.int32)
    return {"prompt_hidden": prompt_hidden, "qkv_weight": qkv_weight, "out_weight": out_weight, "embed_table": embed_table, "response_ids": response_ids, "assignment": assignment}


def rms_rows(values):
    return values * lax.rsqrt(lax.optimization_barrier(jnp.mean(values * values, axis=-1, keepdims=True)) + 1e-06)

def reference(prompt_hidden, qkv_weight, out_weight, embed_table, response_ids, assignment):
    kv_weight = jnp.concatenate([qkv_weight[1], qkv_weight[2]], axis=1)
    rows = prompt_hidden.reshape(2 * PLEN, D)
    kv_all = jnp.dot(rows, kv_weight, preferred_element_type=jnp.float32).astype(jnp.bfloat16)
    kv_all = kv_all.reshape(2, PLEN, 2, H, DH)
    keys = kv_all[:, :, 0].astype(jnp.float32)
    values = kv_all[:, :, 1].astype(jnp.float32)
    state = jnp.einsum('pthd,pthe->phde', keys, values)
    embedded = jnp.take(embed_table, response_ids, axis=0)
    normed = rms_rows(embedded.astype(jnp.float32)).astype(jnp.bfloat16)
    flat = normed.reshape(STEPS * RESP, D)
    query = jnp.dot(flat, qkv_weight[0], preferred_element_type=jnp.float32).astype(jnp.bfloat16).reshape(STEPS, RESP, H, DH)
    key = jnp.dot(flat, qkv_weight[1], preferred_element_type=jnp.float32).astype(jnp.bfloat16).reshape(STEPS, RESP, H, DH)
    value = jnp.dot(flat, qkv_weight[2], preferred_element_type=jnp.float32).astype(jnp.bfloat16).reshape(STEPS, RESP, H, DH)
    query_f = query.astype(jnp.float32)
    both = jnp.einsum('trhd,phde->ptrhe', query_f, state, precision=lax.Precision.HIGHEST)
    chosen = jnp.where((assignment == 0)[None, :, None, None], both[0], both[1])
    scores = jnp.einsum('trhd,srhd->rhts', query_f, key.astype(jnp.float32))
    later = jnp.arange(STEPS)[:, None] >= jnp.arange(STEPS)[None, :]
    scores = jnp.where(later[None, None], scores, 0.0).astype(jnp.bfloat16)
    local = jnp.einsum('rhts,srhd->trhd', scores.astype(jnp.float32), value.astype(jnp.float32))
    attended = chosen + local
    head_out = rms_rows(attended).astype(jnp.bfloat16).reshape(STEPS * RESP, D)
    projected = jnp.dot(head_out, out_weight, preferred_element_type=jnp.float32).reshape(STEPS, RESP, D)
    mixed = embedded.astype(jnp.float32) + projected
    return rms_rows(mixed).astype(jnp.bfloat16)
```

```python
import functools

import jax
import jax.numpy as jnp
from jax import lax
from jax.experimental import pallas as pl
from jax.experimental.pallas import tpu as pltpu
from jax.sharding import PartitionSpec as P

DH = 128
SUB = 2
MESH = pl.DeviceIdType.MESH


def rms_rows(values):
    return values * lax.rsqrt(jnp.mean(values * values, axis=-1, keepdims=True) + 1e-06)


def remote(src, dst, send, recv, target):
    return pltpu.make_async_remote_copy(
        src_ref=src, dst_ref=dst, send_sem=send, recv_sem=recv,
        device_id=target, device_id_type=MESH,
    )


def greet(axes):
    barrier = pltpu.get_barrier_semaphore()
    total = 0
    for axis, size in axes:
        me = lax.axis_index(axis)
        for step in range(1, size):
            pl.semaphore_signal(
                barrier, inc=1, device_id={axis: lax.rem(me + step, size)}, device_id_type=MESH
            )
        total += size - 1
    pl.semaphore_wait(barrier, total)


def gather_kernel(sizes, p_ref, w_ref, o_ref, looked_ref, pf_ref, wf_ref, of_ref, ef_ref, em_ref,
                  e_in, own_sem, e_send, e_recv, z_send, z_recv, x_send, x_recv,
                  y_send, y_recv, pown_send, pown_recv, px_send, px_recv, py_send, py_recv):
    grp_n, ctx_n, head_n = sizes
    chips = ctx_n // 2
    grp, ctx, head = lax.axis_index("grp"), lax.axis_index("ctx"), lax.axis_index("head")
    chip, core = ctx // 2, lax.rem(ctx, 2)
    partner = {"ctx": chip * 2 + 1 - core}
    kinds, rows, cols = w_ref.shape
    o_rows, o_cols = o_ref.shape
    width = p_ref.shape[2]
    resp = em_ref.shape[1]
    w_sub = rows // (grp_n * SUB)
    o_sub = o_rows // (grp_n * SUB)
    chunks = [(kind, sub) for kind in (1, 2, 0, 3) for sub in range(SUB)]

    def chunk_dst(index, shard, part):
        kind, sub = chunks[index]
        if kind == 3:
            start = pl.multiple_of((part * SUB + sub) * o_sub, o_sub)
            return of_ref.at[pl.ds(start, o_sub), pl.ds(pl.multiple_of(shard * o_cols, o_cols), o_cols)]
        start = pl.multiple_of(shard * rows + (part * SUB + sub) * w_sub, w_sub)
        return wf_ref.at[kind, pl.ds(start, w_sub), :]

    def chunk_src(index, part):
        kind, sub = chunks[index]
        if kind == 3:
            return o_ref.at[pl.ds(pl.multiple_of((part * SUB + sub) * o_sub, o_sub), o_sub), :]
        return w_ref.at[kind, pl.ds(pl.multiple_of((part * SUB + sub) * w_sub, w_sub), w_sub), :]

    def prompt_at(owner):
        return pf_ref.at[:, :, pl.ds(pl.multiple_of(owner * width, width), width)]

    def embed_at(owner):
        return ef_ref.at[:, :, pl.ds(pl.multiple_of(owner * width, width), width)]

    def w_at(shard):
        return wf_ref.at[:, pl.ds(pl.multiple_of(shard * rows, rows), rows), :]

    def o_at(shard):
        return of_ref.at[:, pl.ds(pl.multiple_of(shard * o_cols, o_cols), o_cols)]

    greet((("grp", grp_n), ("ctx", ctx_n), ("head", head_n)))

    ends = []

    def at_end(ok, fn):
        ends.append((ok, fn))

    for step in range(1, ctx_n):
        to = lax.rem(ctx + step, ctx_n)
        copy = remote(
            looked_ref.at[:, pl.ds(pl.multiple_of(to * resp, resp), resp), :], e_in.at[step - 1],
            e_send.at[step - 1], e_recv.at[step - 1], {"ctx": to},
        )
        copy.start()
        at_end(None, copy.wait_send)

    def x_copy(src, index, way, dist, shard):
        return remote(src, chunk_dst(index, shard, grp), x_send.at[way, dist - 1, index],
                      x_recv.at[way, dist - 1, index], {"ctx": ctx + (2 if way == 0 else -2)})

    def z_copy(src, dst, what, way, dist):
        return remote(src, dst, z_send.at[what, way, dist - 1], z_recv.at[what, way, dist - 1],
                      {"head": head + (1 if way == 0 else -1)})

    x_next = (chip + 1 < chips, chip > 0)
    z_next = (head + 1 < head_n, head > 0)

    def start_if(ok, copy):
        pl.when(ok)(copy.start)
        at_end(ok, copy.wait_send)

    for way in range(2):
        start_if(z_next[way], z_copy(p_ref, prompt_at(head), 0, way, 1))
    for index in range(len(chunks)):
        for way in range(2):
            if chips > 1:
                start_if(x_next[way], x_copy(chunk_src(index, grp), index, way, 1, ctx))

    mate = chip * 2 + 1 - core
    for number, (src, dst) in enumerate(((w_ref, w_at), (o_ref, o_at))):
        local = pltpu.make_async_copy(src, dst(ctx), own_sem.at[number])
        local.start()
        at_end(None, local.wait)
        copy = remote(src, dst(ctx), pown_send.at[number], pown_recv.at[number], partner)
        copy.start()
        at_end(None, copy.wait_send)
        at_end(None, remote(src, dst(mate), pown_send.at[number], pown_recv.at[number], partner).wait_recv)
    local = pltpu.make_async_copy(p_ref, prompt_at(head), own_sem.at[2])
    local.start()
    at_end(None, local.wait)

    total = looked_ref[:, pl.ds(pl.multiple_of(ctx * resp, resp), resp), :].astype(jnp.float32)
    for step in range(1, ctx_n):
        remote(e_in.at[step - 1], e_in.at[step - 1], e_send.at[step - 1], e_recv.at[step - 1], partner).wait_recv()
        total += e_in[step - 1].astype(jnp.float32)
    em_ref[...] = total.astype(em_ref.dtype)
    local = pltpu.make_async_copy(em_ref, embed_at(head), own_sem.at[3])
    local.start()
    at_end(None, local.wait)
    for way in range(2):
        start_if(z_next[way], z_copy(em_ref, embed_at(head), 1, way, 1))

    events = []

    def z_event(what, way, dist):
        owner = head - dist if way == 0 else head + dist
        have = owner >= 0 if way == 0 else owner < head_n
        place = (prompt_at, embed_at)[what](owner)

        @pl.when(have)
        def _():
            z_copy(place, place, what, way, dist).wait_recv()

        if dist + 1 < head_n:
            ok = have & z_next[way]
            start_if(ok, z_copy(place, place, what, way, dist + 1))

    for dist in range(1, head_n):
        for way in range(2):
            events.append((22.0 * dist, functools.partial(z_event, 0, way, dist)))
            events.append((22.0 * dist + 5.0, functools.partial(z_event, 1, way, dist)))

    def pass_on(ok, dst, send, recv):
        copy = remote(dst, dst, send, recv, partner)
        start_if(ok, copy)

    def mate_wait(ok, dst, send, recv):
        at_end(ok, remote(dst, dst, send, recv, partner).wait_recv)

    def x_event(index, way, dist):
        from_chip = chip - dist if way == 0 else chip + dist
        have = from_chip >= 0 if way == 0 else from_chip < chips
        place = chunk_dst(index, from_chip * 2 + core, grp)

        @pl.when(have)
        def _():
            x_copy(place, index, way, dist, from_chip * 2 + core).wait_recv()

        if dist + 1 < chips:
            start_if(have & x_next[way], x_copy(place, index, way, dist + 1, from_chip * 2 + core))
        for step in range(1, grp_n):
            start_if(have, remote(place, place, y_send.at[way, dist - 1, step - 1, index],
                                  y_recv.at[way, dist - 1, step - 1, index],
                                  {"grp": lax.rem(grp + step, grp_n)}))
        sems = px_send.at[way, dist - 1, index], px_recv.at[way, dist - 1, index]
        pass_on(have, place, *sems)
        mate_wait(have, chunk_dst(index, from_chip * 2 + 1 - core, grp), *sems)

    def y_event(index, way, dist, step):
        from_chip = chip - dist if way == 0 else chip + dist
        have = from_chip >= 0 if way == 0 else from_chip < chips
        part = lax.rem(grp + grp_n - step, grp_n)
        place = chunk_dst(index, from_chip * 2 + core, part)
        key = (way, dist - 1, step - 1, index)

        @pl.when(have)
        def _():
            remote(place, place, y_send.at[key], y_recv.at[key], partner).wait_recv()

        sems = py_send.at[key], py_recv.at[key]
        pass_on(have, place, *sems)
        mate_wait(have, chunk_dst(index, from_chip * 2 + 1 - core, part), *sems)

    for dist in range(1, chips):
        for index in range(len(chunks)):
            when = 11.0 * (index + 1) + 88.0 * (dist - 1)
            for way in range(2):
                events.append((when, functools.partial(x_event, index, way, dist)))
                for step in range(1, grp_n):
                    events.append((when + 12.0, functools.partial(y_event, index, way, dist, step)))
    for _, fn in sorted(events, key=lambda event: event[0]):
        fn()
    for ok, fn in ends:
        if ok is None:
            fn()
        else:
            pl.when(ok)(fn)


def gather_all(sizes, prompt_hidden, qkv_weight, out_weight, looked):
    grp_n, ctx_n, head_n = sizes
    chips = ctx_n // 2
    kinds, rows, cols = qkv_weight.shape
    steps, resp_all, width = looked.shape
    resp = resp_all // ctx_n
    n_chunks = (kinds + 1) * SUB
    dtype = prompt_hidden.dtype
    vmem = pl.BlockSpec(memory_space=pltpu.VMEM)
    hbm = pl.BlockSpec(memory_space=pl.ANY)
    far = max(chips - 1, 1)
    x_sem = pltpu.SemaphoreType.DMA((2, far, n_chunks))
    y_sem = pltpu.SemaphoreType.DMA((2, far, max(grp_n - 1, 1), n_chunks))
    z_sem = pltpu.SemaphoreType.DMA((2, 2, max(head_n - 1, 1)))
    return pl.pallas_call(
        functools.partial(gather_kernel, sizes),
        out_shape=(
            jax.ShapeDtypeStruct(prompt_hidden.shape[:2] + (width * head_n,), dtype),
            jax.ShapeDtypeStruct((kinds, rows * ctx_n, cols), dtype),
            jax.ShapeDtypeStruct((out_weight.shape[0], out_weight.shape[1] * ctx_n), dtype),
            jax.ShapeDtypeStruct((steps, resp, width * head_n), dtype),
            jax.ShapeDtypeStruct((steps, resp, width), dtype),
        ),
        in_specs=[vmem] * 4,
        out_specs=(hbm, hbm, hbm, hbm, vmem),
        scratch_shapes=[
            pltpu.VMEM((ctx_n - 1, steps, resp, width), dtype),
            pltpu.SemaphoreType.DMA((4,)),
            pltpu.SemaphoreType.DMA((ctx_n - 1,)),
            pltpu.SemaphoreType.DMA((ctx_n - 1,)),
            z_sem, z_sem, x_sem, x_sem, y_sem, y_sem,
            pltpu.SemaphoreType.DMA((2,)), pltpu.SemaphoreType.DMA((2,)),
            x_sem, x_sem, y_sem, y_sem,
        ],
        compiler_params=pltpu.CompilerParams(collective_id=0, has_side_effects=True),
    )(prompt_hidden, qkv_weight, out_weight, looked)


def on_device(sizes, prompt_hidden, qkv_weight, out_weight, embed_table, response_ids, assignment):
    local_cols = prompt_hidden.shape[2]
    prompt_rows = prompt_hidden.shape[1]
    head_size = DH
    local_heads = local_cols // head_size
    steps = response_ids.shape[0]
    resp_local = response_ids.shape[1] // lax.axis_size("ctx")
    ctx_index = lax.axis_index("ctx")
    vocab_rows = embed_table.shape[0]
    offset_ids = response_ids - ctx_index * vocab_rows
    inside = (offset_ids >= 0) & (offset_ids < vocab_rows)
    looked = jnp.take(embed_table, jnp.clip(offset_ids, 0, vocab_rows - 1), axis=0)
    looked = jnp.where(inside[:, :, None], looked, jnp.zeros((), looked.dtype))
    piece, full_rows, full_out, embedded, embedded_mine = gather_all(
        sizes, prompt_hidden, qkv_weight, out_weight, looked
    )
    flat_piece = piece.reshape(2 * prompt_rows, piece.shape[2])
    keys = jnp.dot(flat_piece, full_rows[1], preferred_element_type=jnp.float32)
    keys = keys.astype(jnp.bfloat16).reshape(2, prompt_rows, local_heads, head_size)
    values = jnp.dot(flat_piece, full_rows[2], preferred_element_type=jnp.float32)
    values = values.astype(jnp.bfloat16).reshape(2, prompt_rows, local_heads, head_size)
    partial_state = jnp.einsum(
        "pthd,pthe->phde", keys, values, preferred_element_type=jnp.float32
    )
    state = lax.psum(partial_state.astype(jnp.bfloat16), "ctx").astype(jnp.float32)
    normed = rms_rows(embedded.astype(jnp.float32)).astype(jnp.bfloat16)
    projected_qkv = jnp.einsum(
        "trd,kde->trke", normed, full_rows, preferred_element_type=jnp.float32
    ).astype(jnp.bfloat16)
    projected_qkv = projected_qkv.reshape(steps, resp_local, 3, local_heads, head_size)
    query = projected_qkv[:, :, 0]
    key = projected_qkv[:, :, 1]
    value = projected_qkv[:, :, 2]
    my_prompt = lax.dynamic_slice_in_dim(assignment, ctx_index * resp_local, resp_local, 0)
    query_f = query.astype(jnp.float32)
    both = jnp.einsum("trhd,phde->ptrhe", query_f, state, precision=lax.Precision.HIGHEST)
    chosen = jnp.where((my_prompt == 0)[None, :, None, None], both[0], both[1])
    scores = jnp.einsum("trhd,srhd->rhts", query, key, preferred_element_type=jnp.float32)
    later = jnp.arange(steps)[:, None] >= jnp.arange(steps)[None, :]
    scores = jnp.where(later[None, None], scores, 0.0).astype(jnp.bfloat16)
    local = jnp.einsum("rhts,srhd->trhd", scores, value, preferred_element_type=jnp.float32)
    head_out = rms_rows(chosen + local).astype(jnp.bfloat16).reshape(steps, resp_local, local_cols)
    terms = jnp.einsum("trd,de->tre", head_out, full_out, preferred_element_type=jnp.float32)
    width = terms.shape[2]
    mine = lax.psum_scatter(
        terms.astype(jnp.bfloat16), "head", scatter_dimension=2, tiled=True
    ).astype(jnp.float32)
    mixed = embedded_mine.astype(jnp.float32) + mine
    squares = lax.psum(jnp.sum(mixed * mixed, axis=-1), "head")
    result = mixed * lax.rsqrt(squares[:, :, None] / width + 1e-06)
    return result.astype(jnp.bfloat16)


def solution(mesh):
    sizes = (mesh.shape["grp"], mesh.shape["ctx"], mesh.shape["head"])
    return jax.shard_map(
        functools.partial(on_device, sizes),
        mesh=mesh,
        in_specs=(
            P("grp", "ctx", "head"),
            P(None, "ctx", "head"),
            P("head", "ctx"),
            P("ctx", "head"),
            P(None, "grp"),
            P("grp"),
        ),
        out_specs=P(None, ("grp", "ctx"), "head"),
        check_vma=False,
    )
```

```python
import functools

import jax
import jax.numpy as jnp
from jax import lax
from jax.experimental import pallas as pl
from jax.experimental.pallas import tpu as pltpu
from jax.sharding import PartitionSpec as P

DH = 128
SUB = 2
MESH = pl.DeviceIdType.MESH


def rms_rows(values):
    return values * lax.rsqrt(jnp.mean(values * values, axis=-1, keepdims=True) + 1e-06)


def remote(src, dst, send, recv, target):
    return pltpu.make_async_remote_copy(
        src_ref=src, dst_ref=dst, send_sem=send, recv_sem=recv,
        device_id=target, device_id_type=MESH,
    )


def greet(axes):
    barrier = pltpu.get_barrier_semaphore()
    total = 0
    for axis, size in axes:
        me = lax.axis_index(axis)
        for step in range(1, size):
            pl.semaphore_signal(
                barrier, inc=1, device_id={axis: lax.rem(me + step, size)}, device_id_type=MESH
            )
        total += size - 1
    pl.semaphore_wait(barrier, total)


def gather_kernel(sizes, p_ref, w_ref, o_ref, looked_ref, of_ref, em_ref, qkv_ref, state_ref,
                  xa, wf_ref, ef_ref, kv, s_mine, s_chip, s_half, s_mate, s_far, s_back,
                  s_send, s_recv, e_in, own_sem, e_send, e_recv, z_send, z_recv, x_send, x_recv,
                  y_send, y_recv, pown_send, pown_recv, px_send, px_recv, py_send, py_recv):
    grp_n, ctx_n, head_n = sizes
    chips = ctx_n // 2
    grp, ctx, head = lax.axis_index("grp"), lax.axis_index("ctx"), lax.axis_index("head")
    chip, core = ctx // 2, lax.rem(ctx, 2)
    partner = {"ctx": chip * 2 + 1 - core}
    kinds, rows, cols = w_ref.shape
    o_rows, o_cols = o_ref.shape
    p_rows, width = p_ref.shape
    steps, resp = em_ref.shape[:2]
    r_rows = steps * resp
    heads = cols // DH
    tile = min(256, cols)
    w_sub = rows // (grp_n * SUB)
    o_sub = o_rows // (grp_n * SUB)
    chunks = [(kind, sub) for kind in (1, 2, 0, 3) for sub in range(SUB)]

    def chunk_dst(index, shard, part):
        kind, sub = chunks[index]
        if kind == 3:
            start = pl.multiple_of((part * SUB + sub) * o_sub, o_sub)
            return of_ref.at[pl.ds(start, o_sub), pl.ds(pl.multiple_of(shard * o_cols, o_cols), o_cols)]
        start = pl.multiple_of(shard * rows + (part * SUB + sub) * w_sub, w_sub)
        return wf_ref.at[kind, pl.ds(start, w_sub), :]

    def chunk_src(index, part):
        kind, sub = chunks[index]
        if kind == 3:
            return o_ref.at[pl.ds(pl.multiple_of((part * SUB + sub) * o_sub, o_sub), o_sub), :]
        return w_ref.at[kind, pl.ds(pl.multiple_of((part * SUB + sub) * w_sub, w_sub), w_sub), :]

    def prompt_at(owner):
        return xa.at[pl.ds(0, p_rows), pl.ds(pl.multiple_of(owner * width, width), width)]

    def embed_at(owner):
        return ef_ref.at[:, :, pl.ds(pl.multiple_of(owner * width, width), width)]

    def w_at(shard):
        return wf_ref.at[:, pl.ds(pl.multiple_of(shard * rows, rows), rows), :]

    def o_at(shard):
        return of_ref.at[:, pl.ds(pl.multiple_of(shard * o_cols, o_cols), o_cols)]

    greet((("grp", grp_n), ("ctx", ctx_n), ("head", head_n)))

    ends = []

    def at_end(ok, fn):
        ends.append((ok, fn))

    for step in range(1, ctx_n):
        to = lax.rem(ctx + step, ctx_n)
        copy = remote(
            looked_ref.at[:, pl.ds(pl.multiple_of(to * resp, resp), resp), :], e_in.at[step - 1],
            e_send.at[step - 1], e_recv.at[step - 1], {"ctx": to},
        )
        copy.start()
        at_end(None, copy.wait_send)

    def x_copy(src, index, way, dist, shard):
        return remote(src, chunk_dst(index, shard, grp), x_send.at[way, dist - 1, index],
                      x_recv.at[way, dist - 1, index], {"ctx": ctx + (2 if way == 0 else -2)})

    def z_copy(src, dst, what, way, dist):
        return remote(src, dst, z_send.at[what, way, dist - 1], z_recv.at[what, way, dist - 1],
                      {"head": head + (1 if way == 0 else -1)})

    x_next = (chip + 1 < chips, chip > 0)
    z_next = (head + 1 < head_n, head > 0)

    def start_if(ok, copy):
        pl.when(ok)(copy.start)
        at_end(ok, copy.wait_send)

    for way in range(2):
        start_if(z_next[way], z_copy(p_ref, prompt_at(head), 0, way, 1))
    def x_first(index):
        for way in range(2):
            if chips > 1:
                start_if(x_next[way], x_copy(chunk_src(index, grp), index, way, 1, ctx))

    for index in range(len(chunks) - 1):
        x_first(index)

    mate = chip * 2 + 1 - core
    w_ready, x_ready, ef_ready = [], [], []
    for number, (src, dst, ready) in enumerate(((w_ref, w_at, w_ready), (o_ref, o_at, ends))):
        local = pltpu.make_async_copy(src, dst(ctx), own_sem.at[number])
        local.start()
        ready.append((None, local.wait))
        copy = remote(src, dst(ctx), pown_send.at[number], pown_recv.at[number], partner)
        copy.start()
        at_end(None, copy.wait_send)
        ready.append((None, remote(src, dst(mate), pown_send.at[number], pown_recv.at[number], partner).wait_recv))
    local = pltpu.make_async_copy(p_ref, prompt_at(head), own_sem.at[2])
    local.start()
    x_ready.append((None, local.wait))

    def settle(waits):
        for ok, fn in waits:
            if ok is None:
                fn()
            else:
                pl.when(ok)(fn)
        waits.clear()

    total = looked_ref[:, pl.ds(pl.multiple_of(ctx * resp, resp), resp), :].astype(jnp.float32)
    for step in range(1, ctx_n):
        remote(e_in.at[step - 1], e_in.at[step - 1], e_send.at[step - 1], e_recv.at[step - 1], partner).wait_recv()
        total += e_in[step - 1].astype(jnp.float32)
    em_ref[...] = total.astype(em_ref.dtype)
    local = pltpu.make_async_copy(em_ref, embed_at(head), own_sem.at[3])
    local.start()
    ef_ready.append((None, local.wait))
    for way in range(2):
        start_if(z_next[way], z_copy(em_ref, embed_at(head), 1, way, 1))

    events = []

    def z_event(what, way, dist):
        owner = head - dist if way == 0 else head + dist
        have = owner >= 0 if way == 0 else owner < head_n
        place = (prompt_at, embed_at)[what](owner)

        @pl.when(have)
        def _():
            z_copy(place, place, what, way, dist).wait_recv()

        if dist + 1 < head_n:
            ok = have & z_next[way]
            start_if(ok, z_copy(place, place, what, way, dist + 1))

    for dist in range(1, head_n):
        for way in range(2):
            events.append((22.0 * dist, functools.partial(z_event, 0, way, dist)))
            events.append((22.0 * dist + 5.0, functools.partial(z_event, 1, way, dist)))

    def pass_on(ok, dst, send, recv):
        copy = remote(dst, dst, send, recv, partner)
        start_if(ok, copy)

    mate_ready = {kind: [] for kind in range(4)}

    def mate_wait(index, ok, dst, send, recv):
        mate_ready[chunks[index][0]].append((ok, remote(dst, dst, send, recv, partner).wait_recv))

    def x_event(index, way, dist):
        from_chip = chip - dist if way == 0 else chip + dist
        have = from_chip >= 0 if way == 0 else from_chip < chips
        place = chunk_dst(index, from_chip * 2 + core, grp)

        @pl.when(have)
        def _():
            x_copy(place, index, way, dist, from_chip * 2 + core).wait_recv()

        if dist + 1 < chips:
            start_if(have & x_next[way], x_copy(place, index, way, dist + 1, from_chip * 2 + core))
        for step in range(1, grp_n):
            start_if(have, remote(place, place, y_send.at[way, dist - 1, step - 1, index],
                                  y_recv.at[way, dist - 1, step - 1, index],
                                  {"grp": lax.rem(grp + step, grp_n)}))
        sems = px_send.at[way, dist - 1, index], px_recv.at[way, dist - 1, index]
        pass_on(have, place, *sems)
        mate_wait(index, have, chunk_dst(index, from_chip * 2 + 1 - core, grp), *sems)

    def y_event(index, way, dist, step):
        from_chip = chip - dist if way == 0 else chip + dist
        have = from_chip >= 0 if way == 0 else from_chip < chips
        part = lax.rem(grp + grp_n - step, grp_n)
        place = chunk_dst(index, from_chip * 2 + core, part)
        key = (way, dist - 1, step - 1, index)

        @pl.when(have)
        def _():
            remote(place, place, y_send.at[key], y_recv.at[key], partner).wait_recv()

        sems = py_send.at[key], py_recv.at[key]
        pass_on(have, place, *sems)
        mate_wait(index, have, chunk_dst(index, from_chip * 2 + 1 - core, part), *sems)

    def norm_rows():
        settle(ef_ready)
        values = ef_ref[...].astype(jnp.float32).reshape(r_rows, ef_ref.shape[2])
        xa[pl.ds(p_rows, r_rows), :] = rms_rows(values).astype(xa.dtype)

    def project(kind, first, last):
        settle(x_ready)
        if kind == 1 and first == 0:
            settle(w_ready)
        settle(mate_ready[kind])

        @pl.loop(first, last)
        def _(number):
            lanes = pl.ds(pl.multiple_of(number * tile, tile), tile)
            if kind == 0:
                rows_in = xa[pl.ds(p_rows, r_rows), :]
            else:
                rows_in = xa[...]
            out = jnp.dot(rows_in, wf_ref[kind, :, lanes], preferred_element_type=jnp.float32)
            out = out.astype(kv.dtype)
            if kind == 0:
                qkv_ref[0, :, lanes] = out
            else:
                kv[kind - 1, :, lanes] = out[:p_rows]
                qkv_ref[kind, :, lanes] = out[p_rows:]

    def to_mate(src, dst, number):
        return remote(src, dst, s_send.at[number], s_recv.at[number], partner)

    def make_state():
        span = p_rows // 2

        @pl.loop(0, 2 * heads)
        def _(number):
            rows_at = pl.ds(pl.multiple_of(number // heads * span, span), span)
            lanes = pl.ds(pl.multiple_of(lax.rem(number, heads) * DH, DH), DH)
            s_chip[number] = lax.dot_general(
                kv[0, rows_at, lanes], kv[1, rows_at, lanes], (((0,), (0,)), ((), ())),
                preferred_element_type=jnp.float32,
            )
        s_mine[...] = s_chip[...].astype(s_mine.dtype)
        copy = to_mate(s_mine, s_mate, 0)
        copy.start()
        at_end(None, copy.wait_send)

    mine = pl.ds(core * heads, heads)
    theirs = pl.ds((1 - core) * heads, heads)

    def far_copy(step):
        other = lax.rem(chip + step, chips)
        return remote(s_half, s_far.at[step - 1], s_send.at[1 + step], s_recv.at[1 + step],
                      {"ctx": other * 2 + core})

    def chip_state():
        to_mate(s_mine, s_mate, 0).wait_recv()
        s_chip[...] = s_chip[...] + s_mate[...].astype(jnp.float32)
        s_half[...] = s_chip[mine].astype(s_half.dtype)
        for step in range(1, chips):
            copy = far_copy(step)
            copy.start()
            at_end(None, copy.wait_send)
        x_first(len(chunks) - 1)

    def whole_state():
        total = s_chip[mine]
        for step in range(1, chips):
            far_copy(step).wait_recv()
            total = total + s_far[step - 1].astype(jnp.float32)
        state_ref[mine] = total
        s_back[0] = total.astype(s_back.dtype)
        copy = to_mate(s_back.at[0], s_back.at[1], 1)
        copy.start()
        at_end(None, copy.wait_send)

    def mate_state():
        to_mate(s_back.at[0], s_back.at[1], 1).wait_recv()
        state_ref[theirs] = s_back[1].astype(jnp.float32)

    ready = 22.0 * (head_n - 1) + 5.5
    for dist in range(1, chips):
        ready = max(ready, 11.0 * 2 * SUB + 12.5 + 88.0 * (dist - 1))
    after = ready + 20.0
    for dist in range(1, chips):
        for index in range(len(chunks)):
            when = 11.0 * (index + 1) + 88.0 * (dist - 1)
            if index == len(chunks) - 1:
                when = max(when, after + 12.0 * dist)
            for way in range(2):
                events.append((when, functools.partial(x_event, index, way, dist)))
                for step in range(1, grp_n):
                    events.append((when + 12.0, functools.partial(y_event, index, way, dist, step)))
    tiles = cols // tile
    cut = (tiles + 1) // 2
    events.append((ready, norm_rows))
    for number, kind in enumerate((1, 2)):
        events.append((ready + 10.0 * number, functools.partial(project, kind, 0, cut)))
        if cut < tiles:
            events.append((ready + 10.0 * number + 5.0, functools.partial(project, kind, cut, tiles)))
    events.append((after, make_state))
    events.append((after + 2.0, chip_state))
    last = max(when for when, _ in events)
    events.append((max(after + 3.0, 11.0 * 3 * SUB + 12.5 + 88.0 * max(chips - 2, 0)),
                   functools.partial(project, 0, 0, tiles)))
    events.append((after + 9.0, whole_state))
    events.append((last + 50.0, mate_state))
    for _, fn in sorted(events, key=lambda event: event[0]):
        fn()
    settle(mate_ready[3])
    settle(ends)


def gather_all(sizes, prompt_hidden, qkv_weight, out_weight, looked):
    grp_n, ctx_n, head_n = sizes
    chips = ctx_n // 2
    kinds, rows, cols = qkv_weight.shape
    steps, resp_all, width = looked.shape
    resp = resp_all // ctx_n
    p_rows = prompt_hidden.shape[0]
    heads = cols // DH
    features = width * head_n
    n_chunks = (kinds + 1) * SUB
    dtype = prompt_hidden.dtype
    vmem = pl.BlockSpec(memory_space=pltpu.VMEM)
    hbm = pl.BlockSpec(memory_space=pl.ANY)
    far = max(chips - 1, 1)
    x_sem = pltpu.SemaphoreType.DMA((2, far, n_chunks))
    y_sem = pltpu.SemaphoreType.DMA((2, far, max(grp_n - 1, 1), n_chunks))
    z_sem = pltpu.SemaphoreType.DMA((2, 2, max(head_n - 1, 1)))
    s_sem = pltpu.SemaphoreType.DMA((1 + chips,))
    return pl.pallas_call(
        functools.partial(gather_kernel, sizes),
        out_shape=(
            jax.ShapeDtypeStruct((out_weight.shape[0], out_weight.shape[1] * ctx_n), dtype),
            jax.ShapeDtypeStruct((steps, resp, width), dtype),
            jax.ShapeDtypeStruct((kinds, steps * resp, cols), dtype),
            jax.ShapeDtypeStruct((2 * heads, DH, DH), jnp.float32),
        ),
        in_specs=[hbm, hbm, vmem, vmem],
        out_specs=(hbm, vmem, vmem, vmem),
        scratch_shapes=[
            pltpu.VMEM((p_rows + steps * resp, features), dtype),
            pltpu.VMEM((kinds, rows * ctx_n, cols), dtype),
            pltpu.VMEM((steps, resp, features), dtype),
            pltpu.VMEM((2, p_rows, cols), dtype),
            pltpu.VMEM((2 * heads, DH, DH), dtype),
            pltpu.VMEM((2 * heads, DH, DH), jnp.float32),
            pltpu.VMEM((heads, DH, DH), dtype),
            pltpu.VMEM((2 * heads, DH, DH), dtype),
            pltpu.VMEM((far, heads, DH, DH), dtype),
            pltpu.VMEM((2, heads, DH, DH), dtype),
            s_sem, s_sem,
            pltpu.VMEM((ctx_n - 1, steps, resp, width), dtype),
            pltpu.SemaphoreType.DMA((4,)),
            pltpu.SemaphoreType.DMA((ctx_n - 1,)),
            pltpu.SemaphoreType.DMA((ctx_n - 1,)),
            z_sem, z_sem, x_sem, x_sem, y_sem, y_sem,
            pltpu.SemaphoreType.DMA((2,)), pltpu.SemaphoreType.DMA((2,)),
            x_sem, x_sem, y_sem, y_sem,
        ],
        compiler_params=pltpu.CompilerParams(
            collective_id=0, has_side_effects=True, vmem_limit_bytes=62 * 1024 * 1024
        ),
    )(prompt_hidden, qkv_weight, out_weight, looked)


def finish_kernel(head_n, t_ref, em_ref, out_ref, parts, squares, far_squares,
                  t_send, t_recv, q_send, q_recv):
    head = lax.axis_index("head")
    width = em_ref.shape[2]
    greet((("head", head_n),))

    def block(owner):
        return pl.ds(pl.multiple_of(owner * width, width), width)

    def term_copy(step):
        to = lax.rem(head + step, head_n)
        return remote(t_ref.at[:, :, block(to)], parts.at[step - 1],
                      t_send.at[step - 1], t_recv.at[step - 1], {"head": to})

    def square_copy(step):
        to = lax.rem(head + step, head_n)
        return remote(squares, far_squares.at[step - 1],
                      q_send.at[step - 1], q_recv.at[step - 1], {"head": to})

    for step in range(1, head_n):
        term_copy(step).start()
    mixed = em_ref[...].astype(jnp.float32) + t_ref[:, :, block(head)].astype(jnp.float32)
    for step in range(1, head_n):
        term_copy(step).wait_recv()
        mixed += parts[step - 1].astype(jnp.float32)
    total = jnp.broadcast_to(jnp.sum(mixed * mixed, axis=-1, keepdims=True), squares.shape)
    squares[...] = total
    for step in range(1, head_n):
        square_copy(step).start()
    for step in range(1, head_n):
        square_copy(step).wait_recv()
        total += far_squares[step - 1]
    scale = lax.rsqrt(total[:, :, :1] / (width * head_n) + 1e-06)
    out_ref[...] = (mixed * scale).astype(out_ref.dtype)
    for step in range(1, head_n):
        term_copy(step).wait_send()
        square_copy(step).wait_send()


def finish(head_n, terms, embedded_mine):
    steps, resp, width = embedded_mine.shape
    vmem = pl.BlockSpec(memory_space=pltpu.VMEM)
    others = max(head_n - 1, 1)
    sem = pltpu.SemaphoreType.DMA((others,))
    return pl.pallas_call(
        functools.partial(finish_kernel, head_n),
        out_shape=jax.ShapeDtypeStruct(embedded_mine.shape, jnp.bfloat16),
        in_specs=[vmem, vmem],
        out_specs=vmem,
        scratch_shapes=[
            pltpu.VMEM((others,) + embedded_mine.shape, jnp.bfloat16),
            pltpu.VMEM((steps, resp, 128), jnp.float32),
            pltpu.VMEM((others, steps, resp, 128), jnp.float32),
            sem, sem, sem, sem,
        ],
        compiler_params=pltpu.CompilerParams(collective_id=1, has_side_effects=True),
    )(terms, embedded_mine)


def on_device(sizes, prompt_hidden, qkv_weight, out_weight, embed_table, response_ids, assignment):
    local_cols = prompt_hidden.shape[2]
    prompt_rows = prompt_hidden.shape[1]
    head_size = DH
    local_heads = local_cols // head_size
    steps = response_ids.shape[0]
    resp_local = response_ids.shape[1] // lax.axis_size("ctx")
    ctx_index = lax.axis_index("ctx")
    vocab_rows = embed_table.shape[0]
    offset_ids = response_ids - ctx_index * vocab_rows
    inside = (offset_ids >= 0) & (offset_ids < vocab_rows)
    looked = jnp.take(embed_table, jnp.clip(offset_ids, 0, vocab_rows - 1), axis=0)
    looked = jnp.where(inside[:, :, None], looked, jnp.zeros((), looked.dtype))
    full_out, embedded_mine, projected_qkv, state = gather_all(
        sizes, prompt_hidden.reshape(2 * prompt_rows, local_cols), qkv_weight, out_weight, looked
    )
    state = state.reshape(2, local_heads, head_size, head_size)
    projected_qkv = projected_qkv.reshape(3, steps, resp_local, local_heads, head_size)
    query = projected_qkv[0]
    key = projected_qkv[1]
    value = projected_qkv[2]
    my_prompt = lax.dynamic_slice_in_dim(assignment, ctx_index * resp_local, resp_local, 0)
    query_f = query.astype(jnp.float32)
    both = jnp.einsum("trhd,phde->ptrhe", query_f, state, precision=lax.Precision.HIGHEST)
    chosen = jnp.where((my_prompt == 0)[None, :, None, None], both[0], both[1])
    scores = jnp.einsum("trhd,srhd->rhts", query, key, preferred_element_type=jnp.float32)
    later = jnp.arange(steps)[:, None] >= jnp.arange(steps)[None, :]
    scores = jnp.where(later[None, None], scores, 0.0).astype(jnp.bfloat16)
    local = jnp.einsum("rhts,srhd->trhd", scores, value, preferred_element_type=jnp.float32)
    head_out = rms_rows(chosen + local).astype(jnp.bfloat16).reshape(steps, resp_local, local_cols)
    terms = jnp.einsum("trd,de->tre", head_out, full_out, preferred_element_type=jnp.float32)
    return finish(sizes[2], terms.astype(jnp.bfloat16), embedded_mine)


def solution(mesh):
    sizes = (mesh.shape["grp"], mesh.shape["ctx"], mesh.shape["head"])
    return jax.shard_map(
        functools.partial(on_device, sizes),
        mesh=mesh,
        in_specs=(
            P("grp", "ctx", "head"),
            P(None, "ctx", "head"),
            P("head", "ctx"),
            P("ctx", "head"),
            P(None, "grp"),
            P("grp"),
        ),
        out_specs=P(None, ("grp", "ctx"), "head"),
        check_vma=False,
    )
```

```python
import functools

import jax
import jax.numpy as jnp
from jax import lax
from jax.experimental import pallas as pl
from jax.experimental.pallas import tpu as pltpu
from jax.sharding import PartitionSpec as P

DH = 128
SUB = 2
MESH = pl.DeviceIdType.MESH


def rms_rows(values):
    return values * lax.rsqrt(jnp.mean(values * values, axis=-1, keepdims=True) + 1e-06)


def remote(src, dst, send, recv, target):
    return pltpu.make_async_remote_copy(
        src_ref=src, dst_ref=dst, send_sem=send, recv_sem=recv,
        device_id=target, device_id_type=MESH,
    )


def greet(axes):
    barrier = pltpu.get_barrier_semaphore()
    total = 0
    for axis, size in axes:
        me = lax.axis_index(axis)
        for step in range(1, size):
            pl.semaphore_signal(
                barrier, inc=1, device_id={axis: lax.rem(me + step, size)}, device_id_type=MESH
            )
        total += size - 1
    pl.semaphore_wait(barrier, total)


def gather_kernel(sizes, p_ref, w_ref, o_ref, ids_ref, table_ref, of_ref, em_ref, qkv_ref, state_ref,
                  xa, wf_ref, ef_ref, acc, found, looked_ref, t_tile, t_sem, s_mine, s_chip, s_half, s_mate, s_far, s_back,
                  s_send, s_recv, e_in, own_sem, e_send, e_recv, z_send, z_recv, x_send, x_recv,
                  y_send, y_recv, pown_send, pown_recv, px_send, px_recv, py_send, py_recv):
    grp_n, ctx_n, head_n = sizes
    chips = ctx_n // 2
    grp, ctx, head = lax.axis_index("grp"), lax.axis_index("ctx"), lax.axis_index("head")
    chip, core = ctx // 2, lax.rem(ctx, 2)
    partner = {"ctx": chip * 2 + 1 - core}
    kinds, rows, cols = w_ref.shape
    o_rows, o_cols = o_ref.shape
    p_rows, width = p_ref.shape
    steps, resp = em_ref.shape[:2]
    r_rows = steps * resp
    heads = cols // DH
    tile = min(256, cols)
    tiles = cols // tile
    w_sub = rows // (grp_n * SUB)
    o_sub = o_rows // (grp_n * SUB)
    chunks = [(kind, sub) for kind in (1, 2, 0, 3) for sub in range(SUB)]

    def chunk_dst(index, shard, part):
        kind, sub = chunks[index]
        if kind == 3:
            start = pl.multiple_of((part * SUB + sub) * o_sub, o_sub)
            return of_ref.at[pl.ds(start, o_sub), pl.ds(pl.multiple_of(shard * o_cols, o_cols), o_cols)]
        start = pl.multiple_of(shard * rows + (part * SUB + sub) * w_sub, w_sub)
        return wf_ref.at[kind, pl.ds(start, w_sub), :]

    def chunk_src(index, part):
        kind, sub = chunks[index]
        if kind == 3:
            return o_ref.at[pl.ds(pl.multiple_of((part * SUB + sub) * o_sub, o_sub), o_sub), :]
        return w_ref.at[kind, pl.ds(pl.multiple_of((part * SUB + sub) * w_sub, w_sub), w_sub), :]

    def prompt_at(owner):
        return xa.at[pl.ds(0, p_rows), pl.ds(pl.multiple_of(owner * width, width), width)]

    def embed_at(owner):
        return ef_ref.at[:, :, pl.ds(pl.multiple_of(owner * width, width), width)]

    def w_at(shard):
        return wf_ref.at[:, pl.ds(pl.multiple_of(shard * rows, rows), rows), :]

    def o_at(shard):
        return of_ref.at[:, pl.ds(pl.multiple_of(shard * o_cols, o_cols), o_cols)]

    greet((("grp", grp_n), ("ctx", ctx_n), ("head", head_n)))

    ends = []

    def at_end(ok, fn):
        ends.append((ok, fn))

    def x_copy(src, index, way, dist, shard):
        return remote(src, chunk_dst(index, shard, grp), x_send.at[way, dist - 1, index],
                      x_recv.at[way, dist - 1, index], {"ctx": ctx + (2 if way == 0 else -2)})

    def z_copy(src, dst, what, way, dist):
        return remote(src, dst, z_send.at[what, way, dist - 1], z_recv.at[what, way, dist - 1],
                      {"head": head + (1 if way == 0 else -1)})

    x_next = (chip + 1 < chips, chip > 0)
    z_next = (head + 1 < head_n, head > 0)

    def start_if(ok, copy):
        pl.when(ok)(copy.start)
        at_end(ok, copy.wait_send)

    for way in range(2):
        start_if(z_next[way], z_copy(p_ref, prompt_at(head), 0, way, 1))
    def x_first(index):
        for way in range(2):
            if chips > 1:
                start_if(x_next[way], x_copy(chunk_src(index, grp), index, way, 1, ctx))

    for index in range(2):
        x_first(index)

    mate = chip * 2 + 1 - core
    w_ready, x_ready, ef_ready = [], [], []
    for number, (src, dst, ready) in enumerate(((w_ref, w_at, w_ready), (o_ref, o_at, ends))):
        local = pltpu.make_async_copy(src, dst(ctx), own_sem.at[number])
        local.start()
        ready.append((None, local.wait))
        copy = remote(src, dst(ctx), pown_send.at[number], pown_recv.at[number], partner)
        copy.start()
        at_end(None, copy.wait_send)
        ready.append((None, remote(src, dst(mate), pown_send.at[number], pown_recv.at[number], partner).wait_recv))
    local = pltpu.make_async_copy(p_ref, prompt_at(head), own_sem.at[2])
    local.start()
    x_ready.append((None, local.wait))

    def settle(waits):
        for ok, fn in waits:
            if ok is None:
                fn()
            else:
                pl.when(ok)(fn)
        waits.clear()

    events = []

    vocab = table_ref.shape[0]
    t_rows = t_tile.shape[1]
    n_tiles = vocab // t_rows

    def tile_copy(number, slot):
        start = pl.multiple_of(number * t_rows, t_rows)
        return pltpu.make_async_copy(table_ref.at[pl.ds(start, t_rows), :], t_tile.at[slot], t_sem.at[slot])

    def lookup(first, last):
        tile_copy(first, first % 2).start()
        if first == 0:
            found[...] = jnp.zeros_like(found)

        @pl.loop(first, last)
        def _(number):
            slot = lax.rem(number, 2)

            @pl.when(number + 1 < last)
            def _():
                tile_copy(number + 1, lax.rem(number + 1, 2)).start()

            tile_copy(number, slot).wait()
            names = lax.broadcasted_iota(jnp.int32, (ids_ref.shape[0], t_rows), 1)
            hits = ids_ref[...] == names + (ctx * vocab + number * t_rows)
            pick = jnp.where(hits, 1.0, 0.0).astype(looked_ref.dtype)
            found[...] += jnp.dot(pick, t_tile[slot], preferred_element_type=jnp.float32)

    def embed_send():
        looked_ref[...] = found[...].astype(looked_ref.dtype).reshape(looked_ref.shape)
        for step in range(1, ctx_n):
            to = lax.rem(ctx + step, ctx_n)
            copy = remote(
                looked_ref.at[:, pl.ds(pl.multiple_of(to * resp, resp), resp), :], e_in.at[step - 1],
                e_send.at[step - 1], e_recv.at[step - 1], {"ctx": to},
            )
            copy.start()
            at_end(None, copy.wait_send)
        x_first(2)

    def embed_sum():
        total = looked_ref[:, pl.ds(pl.multiple_of(ctx * resp, resp), resp), :].astype(jnp.float32)
        for step in range(1, ctx_n):
            remote(e_in.at[step - 1], e_in.at[step - 1], e_send.at[step - 1], e_recv.at[step - 1], partner).wait_recv()
            total += e_in[step - 1].astype(jnp.float32)
        em_ref[...] = total.astype(em_ref.dtype)
        local = pltpu.make_async_copy(em_ref, embed_at(head), own_sem.at[3])
        local.start()
        ef_ready.append((None, local.wait))
        for way in range(2):
            start_if(z_next[way], z_copy(em_ref, embed_at(head), 1, way, 1))

    def z_event(what, way, dist):
        owner = head - dist if way == 0 else head + dist
        have = owner >= 0 if way == 0 else owner < head_n
        place = (prompt_at, embed_at)[what](owner)

        @pl.when(have)
        def _():
            z_copy(place, place, what, way, dist).wait_recv()

        if dist + 1 < head_n:
            ok = have & z_next[way]
            start_if(ok, z_copy(place, place, what, way, dist + 1))

    for dist in range(1, head_n):
        for way in range(2):
            events.append((22.0 * dist, functools.partial(z_event, 0, way, dist)))
            events.append((22.0 * dist + 20.0, functools.partial(z_event, 1, way, dist)))

    def pass_on(ok, dst, send, recv):
        copy = remote(dst, dst, send, recv, partner)
        start_if(ok, copy)

    mate_ready = {kind: [] for kind in range(4)}

    def mate_wait(index, ok, dst, send, recv):
        mate_ready[chunks[index][0]].append((ok, remote(dst, dst, send, recv, partner).wait_recv))

    def x_event(index, way, dist):
        from_chip = chip - dist if way == 0 else chip + dist
        have = from_chip >= 0 if way == 0 else from_chip < chips
        place = chunk_dst(index, from_chip * 2 + core, grp)
        if way == 0 and dist == 1 and 1 <= index < len(chunks) - 2:
            x_first(index + 2)

        @pl.when(have)
        def _():
            x_copy(place, index, way, dist, from_chip * 2 + core).wait_recv()

        if dist + 1 < chips:
            start_if(have & x_next[way], x_copy(place, index, way, dist + 1, from_chip * 2 + core))
        for step in range(1, grp_n):
            start_if(have, remote(place, place, y_send.at[way, dist - 1, step - 1, index],
                                  y_recv.at[way, dist - 1, step - 1, index],
                                  {"grp": lax.rem(grp + step, grp_n)}))
        sems = px_send.at[way, dist - 1, index], px_recv.at[way, dist - 1, index]
        pass_on(have, place, *sems)
        mate_wait(index, have, chunk_dst(index, from_chip * 2 + 1 - core, grp), *sems)

    def y_event(index, way, dist, step):
        from_chip = chip - dist if way == 0 else chip + dist
        have = from_chip >= 0 if way == 0 else from_chip < chips
        part = lax.rem(grp + grp_n - step, grp_n)
        place = chunk_dst(index, from_chip * 2 + core, part)
        key = (way, dist - 1, step - 1, index)

        @pl.when(have)
        def _():
            remote(place, place, y_send.at[key], y_recv.at[key], partner).wait_recv()

        sems = py_send.at[key], py_recv.at[key]
        pass_on(have, place, *sems)
        mate_wait(index, have, chunk_dst(index, from_chip * 2 + 1 - core, part), *sems)

    def norm_rows():
        settle(ef_ready)
        values = ef_ref[...].astype(jnp.float32).reshape(r_rows, ef_ref.shape[2])
        xa[pl.ds(p_rows, r_rows), :] = rms_rows(values).astype(xa.dtype)

    def lanes_of(number):
        return pl.ds(pl.multiple_of(number * tile, tile), tile)

    def prompt_dots(dist):
        settle(x_ready)
        settle(w_ready)
        settle(mate_ready[1])
        settle(mate_ready[2])
        for way in range(2 if dist else 1):
            owner = head - dist if way == 0 else head + dist
            have = owner >= 0 if way == 0 else owner < head_n
            block = pl.ds(pl.multiple_of(owner * width, width), width)

            @pl.when(have)
            def _():
                @pl.loop(0, 2 * tiles)
                def _(number):
                    kind = number // tiles
                    lanes = lanes_of(lax.rem(number, tiles))
                    out = jnp.dot(xa[pl.ds(0, p_rows), block], wf_ref[1 + kind, block, lanes],
                                  preferred_element_type=jnp.float32)
                    if dist:
                        acc[kind, :, lanes] += out
                    else:
                        acc[kind, :, lanes] = out

    def project(kind):
        settle(mate_ready[kind])

        @pl.loop(0, tiles)
        def _(number):
            lanes = lanes_of(number)
            out = jnp.dot(xa[pl.ds(p_rows, r_rows), :], wf_ref[kind, :, lanes],
                          preferred_element_type=jnp.float32)
            qkv_ref[kind, :, lanes] = out.astype(qkv_ref.dtype)

    def to_mate(src, dst, number):
        return remote(src, dst, s_send.at[number], s_recv.at[number], partner)

    def make_state():
        span = p_rows // 2

        @pl.loop(0, 2 * heads)
        def _(number):
            rows_at = pl.ds(pl.multiple_of(number // heads * span, span), span)
            lanes = pl.ds(pl.multiple_of(lax.rem(number, heads) * DH, DH), DH)
            s_chip[number] = lax.dot_general(
                acc[0, rows_at, lanes].astype(s_mine.dtype), acc[1, rows_at, lanes].astype(s_mine.dtype), (((0,), (0,)), ((), ())),
                preferred_element_type=jnp.float32,
            )
        s_mine[...] = s_chip[...].astype(s_mine.dtype)
        copy = to_mate(s_mine, s_mate, 0)
        copy.start()
        at_end(None, copy.wait_send)

    mine = pl.ds(core * heads, heads)
    theirs = pl.ds((1 - core) * heads, heads)

    def far_copy(step):
        other = lax.rem(chip + step, chips)
        return remote(s_half, s_far.at[step - 1], s_send.at[1 + step], s_recv.at[1 + step],
                      {"ctx": other * 2 + core})

    def chip_state():
        to_mate(s_mine, s_mate, 0).wait_recv()
        s_chip[...] = s_chip[...] + s_mate[...].astype(jnp.float32)
        s_half[...] = s_chip[mine].astype(s_half.dtype)
        for step in range(1, chips):
            copy = far_copy(step)
            copy.start()
            at_end(None, copy.wait_send)

    def whole_state():
        total = s_chip[mine]
        for step in range(1, chips):
            far_copy(step).wait_recv()
            total = total + s_far[step - 1].astype(jnp.float32)
        state_ref[mine] = total
        s_back[0] = total.astype(s_back.dtype)
        copy = to_mate(s_back.at[0], s_back.at[1], 1)
        copy.start()
        at_end(None, copy.wait_send)

    def mate_state():
        to_mate(s_back.at[0], s_back.at[1], 1).wait_recv()
        state_ref[theirs] = s_back[1].astype(jnp.float32)

    def reach(chunk):
        return 11.0 * (chunk + 1) + 88.0 * max(chips - 2, 0) + 12.5

    middle = n_tiles // 2
    events.append((0.0, functools.partial(lookup, 0, middle)))
    events.append((11.5, functools.partial(lookup, middle, n_tiles)))
    events.append((11.6, embed_send))
    events.append((30.0, embed_sum))
    for dist in range(1, chips):
        for index in range(len(chunks)):
            when = 11.0 * (index + 1) + 88.0 * (dist - 1)
            for way in range(2):
                events.append((when, functools.partial(x_event, index, way, dist)))
                for step in range(1, grp_n):
                    events.append((when + 12.0, functools.partial(y_event, index, way, dist, step)))
    ready = reach(2 * SUB - 1)
    after = ready
    for dist in range(head_n):
        after = max(ready + 0.1 * dist, 22.0 * dist + 0.5)
        events.append((after, functools.partial(prompt_dots, dist)))
    embedded_at = 22.0 * (head_n - 1) + 20.5
    events.append((after + 0.1, make_state))
    events.append((after + 0.2, chip_state))
    after = max(after + 0.3, embedded_at)
    events.append((after, norm_rows))
    events.append((after + 0.2, functools.partial(project, 1)))
    events.append((after + 3.0, functools.partial(project, 2)))
    events.append((max(after + 6.0, reach(3 * SUB - 1)), functools.partial(project, 0)))
    events.append((max(after + 12.0, reach(4 * SUB - 1) - 6.0), whole_state))
    last = max(when for when, _ in events)
    events.append((last + 50.0, mate_state))
    for _, fn in sorted(events, key=lambda event: event[0]):
        fn()
    settle(mate_ready[3])
    settle(ends)


def gather_all(sizes, prompt_hidden, qkv_weight, out_weight, response_ids, embed_table):
    grp_n, ctx_n, head_n = sizes
    chips = ctx_n // 2
    kinds, rows, cols = qkv_weight.shape
    steps, resp_all = response_ids.shape
    width = prompt_hidden.shape[1]
    resp = resp_all // ctx_n
    p_rows = prompt_hidden.shape[0]
    heads = cols // DH
    features = width * head_n
    n_chunks = (kinds + 1) * SUB
    dtype = prompt_hidden.dtype
    vmem = pl.BlockSpec(memory_space=pltpu.VMEM)
    hbm = pl.BlockSpec(memory_space=pl.ANY)
    far = max(chips - 1, 1)
    x_sem = pltpu.SemaphoreType.DMA((2, far, n_chunks))
    y_sem = pltpu.SemaphoreType.DMA((2, far, max(grp_n - 1, 1), n_chunks))
    z_sem = pltpu.SemaphoreType.DMA((2, 2, max(head_n - 1, 1)))
    s_sem = pltpu.SemaphoreType.DMA((1 + chips,))
    return pl.pallas_call(
        functools.partial(gather_kernel, sizes),
        out_shape=(
            jax.ShapeDtypeStruct((out_weight.shape[0], out_weight.shape[1] * ctx_n), dtype),
            jax.ShapeDtypeStruct((steps, resp, width), dtype),
            jax.ShapeDtypeStruct((kinds, steps * resp, cols), dtype),
            jax.ShapeDtypeStruct((2 * heads, DH, DH), jnp.float32),
        ),
        in_specs=[hbm, hbm, vmem, vmem, hbm],
        out_specs=(hbm, vmem, vmem, vmem),
        scratch_shapes=[
            pltpu.VMEM((p_rows + steps * resp, features), dtype),
            pltpu.VMEM((kinds, rows * ctx_n, cols), dtype),
            pltpu.VMEM((steps, resp, features), dtype),
            pltpu.VMEM((2, p_rows, cols), jnp.float32),
            pltpu.VMEM((steps * resp_all, width), jnp.float32),
            pltpu.VMEM((steps, resp_all, width), dtype),
            pltpu.VMEM((2, min(512, embed_table.shape[0] // 2), width), dtype),
            pltpu.SemaphoreType.DMA((2,)),
            pltpu.VMEM((2 * heads, DH, DH), dtype),
            pltpu.VMEM((2 * heads, DH, DH), jnp.float32),
            pltpu.VMEM((heads, DH, DH), dtype),
            pltpu.VMEM((2 * heads, DH, DH), dtype),
            pltpu.VMEM((far, heads, DH, DH), dtype),
            pltpu.VMEM((2, heads, DH, DH), dtype),
            s_sem, s_sem,
            pltpu.VMEM((ctx_n - 1, steps, resp, width), dtype),
            pltpu.SemaphoreType.DMA((4,)),
            pltpu.SemaphoreType.DMA((ctx_n - 1,)),
            pltpu.SemaphoreType.DMA((ctx_n - 1,)),
            z_sem, z_sem, x_sem, x_sem, y_sem, y_sem,
            pltpu.SemaphoreType.DMA((2,)), pltpu.SemaphoreType.DMA((2,)),
            x_sem, x_sem, y_sem, y_sem,
        ],
        compiler_params=pltpu.CompilerParams(
            collective_id=0, has_side_effects=True, vmem_limit_bytes=62 * 1024 * 1024
        ),
    )(prompt_hidden, qkv_weight, out_weight, response_ids.reshape(-1, 1), embed_table)


def finish_kernel(head_n, t_ref, em_ref, out_ref, mixed, sums, parts, squares, far_squares,
                  t_send, t_recv, q_send, q_recv):
    head = lax.axis_index("head")
    width = em_ref.shape[2]
    greet((("head", head_n),))
    go = (head + 1 < head_n, head > 0)
    have = (head > 0, head + 1 < head_n)

    def term_copy(src, way, to):
        return remote(src, parts.at[way, to], t_send.at[way, to], t_recv.at[way, to],
                      {"head": head + (1 if way == 0 else -1)})

    def square_copy(step):
        to = lax.rem(head + step, head_n)
        return remote(squares, far_squares.at[step - 1],
                      q_send.at[step - 1], q_recv.at[step - 1], {"head": to})

    order = []
    for step in range(head_n - 1):
        order += [(0, head_n - 1 - step), (1, step)]
    for way, to in order:
        ahead = to > head if way == 0 else to < head
        own = t_ref.at[:, :, pl.ds(to * width, width)]

        @pl.when(ahead & have[way])
        def _():
            term_copy(sums.at[way, to], way, to).wait_recv()
            total = own[...].astype(jnp.float32) + parts[way, to].astype(jnp.float32)
            sums[way, to] = total.astype(sums.dtype)
            term_copy(sums.at[way, to], way, to).start()

        @pl.when(ahead & jnp.logical_not(have[way]))
        def _():
            term_copy(own, way, to).start()

    mixed[...] = em_ref[...].astype(jnp.float32) + t_ref[
        :, :, pl.ds(pl.multiple_of(head * width, width), width)
    ].astype(jnp.float32)
    for way in range(2):
        @pl.when(have[way])
        def _():
            term_copy(sums.at[way, 0], way, head).wait_recv()
            mixed[...] += parts[way, head].astype(jnp.float32)

    values = mixed[...]
    total = jnp.broadcast_to(jnp.sum(values * values, axis=-1, keepdims=True), squares.shape)
    squares[...] = total
    for step in range(1, head_n):
        square_copy(step).start()
    for step in range(1, head_n):
        square_copy(step).wait_recv()
        total += far_squares[step - 1]
    scale = lax.rsqrt(total[:, :, :1] / (width * head_n) + 1e-06)
    out_ref[...] = (values * scale).astype(out_ref.dtype)
    for way, to in order:
        ahead = to > head if way == 0 else to < head

        @pl.when(ahead)
        def _():
            term_copy(sums.at[way, to], way, to).wait_send()
    for step in range(1, head_n):
        square_copy(step).wait_send()


def finish(head_n, terms, embedded_mine):
    steps, resp, width = embedded_mine.shape
    vmem = pl.BlockSpec(memory_space=pltpu.VMEM)
    others = max(head_n - 1, 1)
    sem = pltpu.SemaphoreType.DMA((others,))
    t_sem = pltpu.SemaphoreType.DMA((2, head_n))
    return pl.pallas_call(
        functools.partial(finish_kernel, head_n),
        out_shape=jax.ShapeDtypeStruct(embedded_mine.shape, jnp.bfloat16),
        in_specs=[vmem, vmem],
        out_specs=vmem,
        scratch_shapes=[
            pltpu.VMEM(embedded_mine.shape, jnp.float32),
            pltpu.VMEM((2, head_n) + embedded_mine.shape, jnp.bfloat16),
            pltpu.VMEM((2, head_n) + embedded_mine.shape, jnp.bfloat16),
            pltpu.VMEM((steps, resp, 128), jnp.float32),
            pltpu.VMEM((others, steps, resp, 128), jnp.float32),
            t_sem, t_sem, sem, sem,
        ],
        compiler_params=pltpu.CompilerParams(collective_id=1, has_side_effects=True),
    )(terms, embedded_mine)


def on_device(sizes, prompt_hidden, qkv_weight, out_weight, embed_table, response_ids, assignment):
    local_cols = prompt_hidden.shape[2]
    prompt_rows = prompt_hidden.shape[1]
    head_size = DH
    local_heads = local_cols // head_size
    steps = response_ids.shape[0]
    resp_local = response_ids.shape[1] // lax.axis_size("ctx")
    ctx_index = lax.axis_index("ctx")
    full_out, embedded_mine, projected_qkv, state = gather_all(
        sizes, prompt_hidden.reshape(2 * prompt_rows, local_cols), qkv_weight, out_weight,
        response_ids, embed_table,
    )
    state = state.reshape(2, local_heads, head_size, head_size)
    projected_qkv = projected_qkv.reshape(3, steps, resp_local, local_heads, head_size)
    query = projected_qkv[0]
    key = projected_qkv[1]
    value = projected_qkv[2]
    my_prompt = lax.dynamic_slice_in_dim(assignment, ctx_index * resp_local, resp_local, 0)
    query_f = query.astype(jnp.float32)
    both = jnp.einsum("trhd,phde->ptrhe", query_f, state, precision=lax.Precision.HIGHEST)
    chosen = jnp.where((my_prompt == 0)[None, :, None, None], both[0], both[1])
    scores = jnp.einsum("trhd,srhd->rhts", query, key, preferred_element_type=jnp.float32)
    later = jnp.arange(steps)[:, None] >= jnp.arange(steps)[None, :]
    scores = jnp.where(later[None, None], scores, 0.0).astype(jnp.bfloat16)
    local = jnp.einsum("rhts,srhd->trhd", scores, value, preferred_element_type=jnp.float32)
    head_out = rms_rows(chosen + local).astype(jnp.bfloat16).reshape(steps, resp_local, local_cols)
    terms = jnp.einsum("trd,de->tre", head_out, full_out, preferred_element_type=jnp.float32)
    return finish(sizes[2], terms.astype(jnp.bfloat16), embedded_mine)


def solution(mesh):
    sizes = (mesh.shape["grp"], mesh.shape["ctx"], mesh.shape["head"])
    return jax.shard_map(
        functools.partial(on_device, sizes),
        mesh=mesh,
        in_specs=(
            P("grp", "ctx", "head"),
            P(None, "ctx", "head"),
            P("head", "ctx"),
            P("ctx", "head"),
            P(None, "grp"),
            P("grp"),
        ),
        out_specs=P(None, ("grp", "ctx"), "head"),
        check_vma=False,
    )
```

```python
import functools

import jax
import jax.numpy as jnp
from jax import lax
from jax.experimental import pallas as pl
from jax.experimental.pallas import tpu as pltpu
from jax.sharding import PartitionSpec as P

DH = 128
SUB = 4
MESH = pl.DeviceIdType.MESH


def rms_rows(values):
    return values * lax.rsqrt(jnp.mean(values * values, axis=-1, keepdims=True) + 1e-06)


def remote(src, dst, send, recv, target):
    return pltpu.make_async_remote_copy(
        src_ref=src, dst_ref=dst, send_sem=send, recv_sem=recv,
        device_id=target, device_id_type=MESH,
    )


def greet(axes):
    barrier = pltpu.get_barrier_semaphore()
    total = 0
    for axis, size in axes:
        me = lax.axis_index(axis)
        for step in range(1, size):
            pl.semaphore_signal(
                barrier, inc=1, device_id={axis: lax.rem(me + step, size)}, device_id_type=MESH
            )
        total += size - 1
    pl.semaphore_wait(barrier, total)


def gather_kernel(sizes, p_ref, w_ref, o_ref, ids_ref, table_ref, of_ref, em_ref, qkv_ref, state_ref,
                  xa, wf_ref, ef_ref, acc, found, looked_ref, t_tile, t_sem, s_mine, s_chip, s_half, s_mate, s_far, s_back,
                  s_send, s_recv, e_in, e_out, own_sem, e_send, e_recv, z_send, z_recv, x_send, x_recv,
                  y_send, y_recv, pown_send, pown_recv, px_send, px_recv, py_send, py_recv):
    grp_n, ctx_n, head_n = sizes
    chips = ctx_n // 2
    grp, ctx, head = lax.axis_index("grp"), lax.axis_index("ctx"), lax.axis_index("head")
    chip, core = ctx // 2, lax.rem(ctx, 2)
    partner = {"ctx": chip * 2 + 1 - core}
    kinds, rows, cols = w_ref.shape
    o_rows, o_cols = o_ref.shape
    p_rows, width = p_ref.shape
    steps, resp = em_ref.shape[:2]
    r_rows = steps * resp
    heads = cols // DH
    tile = min(256, cols)
    tiles = cols // tile
    w_sub = rows // (grp_n * SUB)
    o_sub = o_rows // (grp_n * SUB)
    chunks = [(kind, sub) for kind in (1, 2, 0, 3) for sub in range(SUB)]

    def chunk_dst(index, shard, part):
        kind, sub = chunks[index]
        if kind == 3:
            start = pl.multiple_of((part * SUB + sub) * o_sub, o_sub)
            return of_ref.at[pl.ds(start, o_sub), pl.ds(pl.multiple_of(shard * o_cols, o_cols), o_cols)]
        start = pl.multiple_of(shard * rows + (part * SUB + sub) * w_sub, w_sub)
        return wf_ref.at[kind, pl.ds(start, w_sub), :]

    def chunk_src(index, part):
        kind, sub = chunks[index]
        if kind == 3:
            return o_ref.at[pl.ds(pl.multiple_of((part * SUB + sub) * o_sub, o_sub), o_sub), :]
        return w_ref.at[kind, pl.ds(pl.multiple_of((part * SUB + sub) * w_sub, w_sub), w_sub), :]

    def prompt_at(owner):
        return xa.at[pl.ds(0, p_rows), pl.ds(pl.multiple_of(owner * width, width), width)]

    def embed_at(owner):
        return ef_ref.at[:, :, pl.ds(pl.multiple_of(owner * width, width), width)]

    def w_at(shard):
        return wf_ref.at[:, pl.ds(pl.multiple_of(shard * rows, rows), rows), :]

    def o_at(shard):
        return of_ref.at[:, pl.ds(pl.multiple_of(shard * o_cols, o_cols), o_cols)]

    greet((("grp", grp_n), ("ctx", ctx_n), ("head", head_n)))

    ends = []

    def at_end(ok, fn):
        ends.append((ok, fn))

    def x_copy(src, index, way, dist, shard):
        return remote(src, chunk_dst(index, shard, grp), x_send.at[way, dist - 1, index],
                      x_recv.at[way, dist - 1, index], {"ctx": ctx + (2 if way == 0 else -2)})

    def z_copy(src, dst, what, way, dist):
        return remote(src, dst, z_send.at[what, way, dist - 1], z_recv.at[what, way, dist - 1],
                      {"head": head + (1 if way == 0 else -1)})

    x_next = (chip + 1 < chips, chip > 0)
    z_next = (head + 1 < head_n, head > 0)

    def start_if(ok, copy):
        pl.when(ok)(copy.start)
        at_end(ok, copy.wait_send)

    for way in range(2):
        start_if(z_next[way], z_copy(p_ref, prompt_at(head), 0, way, 1))
    def x_first(index):
        for way in range(2):
            if chips > 1:
                start_if(x_next[way], x_copy(chunk_src(index, grp), index, way, 1, ctx))

    for index in range(SUB):
        x_first(index)

    mate = chip * 2 + 1 - core
    w_ready, x_ready, ef_ready = [], [], []
    for number, (src, dst, ready) in enumerate(((w_ref, w_at, w_ready), (o_ref, o_at, ends))):
        local = pltpu.make_async_copy(src, dst(ctx), own_sem.at[number])
        local.start()
        ready.append((None, local.wait))
        copy = remote(src, dst(ctx), pown_send.at[number], pown_recv.at[number], partner)
        copy.start()
        at_end(None, copy.wait_send)
        ready.append((None, remote(src, dst(mate), pown_send.at[number], pown_recv.at[number], partner).wait_recv))
    local = pltpu.make_async_copy(p_ref, prompt_at(head), own_sem.at[2])
    local.start()
    x_ready.append((None, local.wait))

    def settle(waits):
        for ok, fn in waits:
            if ok is None:
                fn()
            else:
                pl.when(ok)(fn)
        waits.clear()

    events = []

    vocab = table_ref.shape[0]
    t_rows = t_tile.shape[1]
    n_tiles = vocab // t_rows

    def tile_copy(number, slot):
        start = pl.multiple_of(number * t_rows, t_rows)
        return pltpu.make_async_copy(table_ref.at[pl.ds(start, t_rows), :], t_tile.at[slot], t_sem.at[slot])

    def lookup(first, last):
        tile_copy(first, first % 2).start()
        if first == 0:
            found[...] = jnp.zeros_like(found)

        @pl.loop(first, last)
        def _(number):
            slot = lax.rem(number, 2)

            @pl.when(number + 1 < last)
            def _():
                tile_copy(number + 1, lax.rem(number + 1, 2)).start()

            tile_copy(number, slot).wait()
            names = lax.broadcasted_iota(jnp.int32, (ids_ref.shape[0], t_rows), 1)
            hits = ids_ref[...] == names + (ctx * vocab + number * t_rows)
            pick = jnp.where(hits, 1.0, 0.0).astype(looked_ref.dtype)
            found[...] += jnp.dot(pick, t_tile[slot], preferred_element_type=jnp.float32)

    def embed_send():
        looked_ref[...] = found[...].astype(looked_ref.dtype).reshape(looked_ref.shape)
        for to in range(chips):
            copy = near_copy(to)
            copy.start()
            at_end(None, copy.wait_send)

    def resp_at(owner):
        return pl.ds(pl.multiple_of(owner * resp, resp), resp)

    def near_copy(to):
        return remote(looked_ref.at[:, resp_at(to * 2 + 1 - core), :], e_in.at[to],
                      e_send.at[to], e_recv.at[to], partner)

    def far_rows(step):
        to = lax.rem(chip + step, chips)
        return remote(e_out.at[step - 1], e_in.at[chips + step - 1], e_send.at[chips + step - 1],
                      e_recv.at[chips + step - 1], {"ctx": to * 2 + core})

    def near_sum(to):
        near_copy(to).wait_recv()
        return looked_ref[:, resp_at(to * 2 + core), :].astype(jnp.float32) + e_in[to].astype(jnp.float32)

    def embed_mid():
        for step in range(1, chips):
            e_out[step - 1] = near_sum(lax.rem(chip + step, chips)).astype(e_out.dtype)
            copy = far_rows(step)
            copy.start()
            at_end(None, copy.wait_send)
        for index in range(SUB, 2 * SUB - 1):
            x_first(index)

    def embed_sum():
        total = near_sum(chip)
        for step in range(1, chips):
            far_rows(step).wait_recv()
            total += e_in[chips + step - 1].astype(jnp.float32)
        em_ref[...] = total.astype(em_ref.dtype)
        local = pltpu.make_async_copy(em_ref, embed_at(head), own_sem.at[3])
        local.start()
        ef_ready.append((None, local.wait))
        for way in range(2):
            start_if(z_next[way], z_copy(em_ref, embed_at(head), 1, way, 1))

    def z_event(what, way, dist):
        owner = head - dist if way == 0 else head + dist
        have = owner >= 0 if way == 0 else owner < head_n
        place = (prompt_at, embed_at)[what](owner)

        @pl.when(have)
        def _():
            z_copy(place, place, what, way, dist).wait_recv()

        if dist + 1 < head_n:
            ok = have & z_next[way]
            start_if(ok, z_copy(place, place, what, way, dist + 1))

    for dist in range(1, head_n):
        for way in range(2):
            events.append((22.0 * dist, functools.partial(z_event, 0, way, dist)))
            events.append((22.0 * dist + 20.0, functools.partial(z_event, 1, way, dist)))

    def pass_on(ok, dst, send, recv):
        copy = remote(dst, dst, send, recv, partner)
        start_if(ok, copy)

    mate_ready = {kind: [] for kind in range(4)}

    def mate_wait(index, ok, dst, send, recv):
        mate_ready[chunks[index][0]].append((ok, remote(dst, dst, send, recv, partner).wait_recv))

    def x_event(index, way, dist):
        from_chip = chip - dist if way == 0 else chip + dist
        have = from_chip >= 0 if way == 0 else from_chip < chips
        place = chunk_dst(index, from_chip * 2 + core, grp)
        if way == 0 and dist == 1 and SUB - 1 <= index < len(chunks) - SUB:
            x_first(index + SUB)

        @pl.when(have)
        def _():
            x_copy(place, index, way, dist, from_chip * 2 + core).wait_recv()

        if dist + 1 < chips:
            start_if(have & x_next[way], x_copy(place, index, way, dist + 1, from_chip * 2 + core))
        for step in range(1, grp_n):
            start_if(have, remote(place, place, y_send.at[way, dist - 1, step - 1, index],
                                  y_recv.at[way, dist - 1, step - 1, index],
                                  {"grp": lax.rem(grp + step, grp_n)}))
        sems = px_send.at[way, dist - 1, index], px_recv.at[way, dist - 1, index]
        pass_on(have, place, *sems)
        mate_wait(index, have, chunk_dst(index, from_chip * 2 + 1 - core, grp), *sems)

    def y_event(index, way, dist, step):
        from_chip = chip - dist if way == 0 else chip + dist
        have = from_chip >= 0 if way == 0 else from_chip < chips
        part = lax.rem(grp + grp_n - step, grp_n)
        place = chunk_dst(index, from_chip * 2 + core, part)
        key = (way, dist - 1, step - 1, index)

        @pl.when(have)
        def _():
            remote(place, place, y_send.at[key], y_recv.at[key], partner).wait_recv()

        sems = py_send.at[key], py_recv.at[key]
        pass_on(have, place, *sems)
        mate_wait(index, have, chunk_dst(index, from_chip * 2 + 1 - core, part), *sems)

    def norm_rows():
        settle(ef_ready)
        values = ef_ref[...].astype(jnp.float32).reshape(r_rows, ef_ref.shape[2])
        xa[pl.ds(p_rows, r_rows), :] = rms_rows(values).astype(xa.dtype)

    def lanes_of(number):
        return pl.ds(pl.multiple_of(number * tile, tile), tile)

    def prompt_dots(dist):
        settle(x_ready)
        settle(w_ready)
        settle(mate_ready[1])
        settle(mate_ready[2])
        for way in range(2 if dist else 1):
            owner = head - dist if way == 0 else head + dist
            have = owner >= 0 if way == 0 else owner < head_n
            block = pl.ds(pl.multiple_of(owner * width, width), width)

            @pl.when(have)
            def _():
                @pl.loop(0, 2 * tiles)
                def _(number):
                    kind = number // tiles
                    lanes = lanes_of(lax.rem(number, tiles))
                    out = jnp.dot(xa[pl.ds(0, p_rows), block], wf_ref[1 + kind, block, lanes],
                                  preferred_element_type=jnp.float32)
                    if dist:
                        acc[kind, :, lanes] += out
                    else:
                        acc[kind, :, lanes] = out

    def project(kind):
        settle(mate_ready[kind])

        @pl.loop(0, tiles)
        def _(number):
            lanes = lanes_of(number)
            out = jnp.dot(xa[pl.ds(p_rows, r_rows), :], wf_ref[kind, :, lanes],
                          preferred_element_type=jnp.float32)
            qkv_ref[kind, :, lanes] = out.astype(qkv_ref.dtype)

    def to_mate(src, dst, number):
        return remote(src, dst, s_send.at[number], s_recv.at[number], partner)

    def make_state():
        span = p_rows // 2

        @pl.loop(0, 2 * heads)
        def _(number):
            rows_at = pl.ds(pl.multiple_of(number // heads * span, span), span)
            lanes = pl.ds(pl.multiple_of(lax.rem(number, heads) * DH, DH), DH)
            s_chip[number] = lax.dot_general(
                acc[0, rows_at, lanes].astype(s_mine.dtype), acc[1, rows_at, lanes].astype(s_mine.dtype), (((0,), (0,)), ((), ())),
                preferred_element_type=jnp.float32,
            )
        s_mine[...] = s_chip[...].astype(s_mine.dtype)
        copy = to_mate(s_mine, s_mate, 0)
        copy.start()
        at_end(None, copy.wait_send)

    mine = pl.ds(core * heads, heads)
    theirs = pl.ds((1 - core) * heads, heads)

    def far_copy(step):
        other = lax.rem(chip + step, chips)
        return remote(s_half, s_far.at[step - 1], s_send.at[1 + step], s_recv.at[1 + step],
                      {"ctx": other * 2 + core})

    def chip_state():
        to_mate(s_mine, s_mate, 0).wait_recv()
        s_chip[...] = s_chip[...] + s_mate[...].astype(jnp.float32)
        s_half[...] = s_chip[mine].astype(s_half.dtype)
        for step in range(1, chips):
            copy = far_copy(step)
            copy.start()
            at_end(None, copy.wait_send)

    def whole_state():
        total = s_chip[mine]
        for step in range(1, chips):
            far_copy(step).wait_recv()
            total = total + s_far[step - 1].astype(jnp.float32)
        state_ref[mine] = total
        s_back[0] = total.astype(s_back.dtype)
        copy = to_mate(s_back.at[0], s_back.at[1], 1)
        copy.start()
        at_end(None, copy.wait_send)

    def mate_state():
        to_mate(s_back.at[0], s_back.at[1], 1).wait_recv()
        state_ref[theirs] = s_back[1].astype(jnp.float32)

    unit = 22.0 / SUB

    def reach(chunk):
        return unit * (chunk + 2) + 88.0 * max(chips - 2, 0) + 1.5

    for part in range(4):
        events.append((unit * part + 0.1 if part else 0.0,
                       functools.partial(lookup, n_tiles * part // 4, n_tiles * (part + 1) // 4)))
    events.append((unit * 3 + 0.2, embed_send))
    events.append((unit * 3 + 0.3, embed_mid))
    events.append((30.0, embed_sum))
    for dist in range(1, chips):
        for index in range(len(chunks)):
            when = unit * (index + 1) + 88.0 * (dist - 1)
            for way in range(2):
                events.append((when, functools.partial(x_event, index, way, dist)))
                for step in range(1, grp_n):
                    events.append((when + unit + 1.0, functools.partial(y_event, index, way, dist, step)))
    ready = reach(2 * SUB - 1)
    after = ready
    for dist in range(head_n):
        after = max(ready + 0.1 * dist, 22.0 * dist + 0.5)
        events.append((after, functools.partial(prompt_dots, dist)))
    embedded_at = 22.0 * (head_n - 1) + 20.5
    events.append((after + 0.1, make_state))
    events.append((after + 0.2, chip_state))
    after = max(after + 0.3, embedded_at)
    events.append((after, norm_rows))
    events.append((after + 0.2, functools.partial(project, 1)))
    events.append((after + 3.0, functools.partial(project, 2)))
    events.append((max(after + 6.0, reach(3 * SUB - 1)), functools.partial(project, 0)))
    events.append((max(after + 12.0, reach(4 * SUB - 1) - 6.0), whole_state))
    last = max(when for when, _ in events)
    events.append((last + 50.0, mate_state))
    for _, fn in sorted(events, key=lambda event: event[0]):
        fn()
    settle(mate_ready[3])
    settle(ends)


def gather_all(sizes, prompt_hidden, qkv_weight, out_weight, response_ids, embed_table):
    grp_n, ctx_n, head_n = sizes
    chips = ctx_n // 2
    kinds, rows, cols = qkv_weight.shape
    steps, resp_all = response_ids.shape
    width = prompt_hidden.shape[1]
    resp = resp_all // ctx_n
    p_rows = prompt_hidden.shape[0]
    heads = cols // DH
    features = width * head_n
    n_chunks = (kinds + 1) * SUB
    dtype = prompt_hidden.dtype
    vmem = pl.BlockSpec(memory_space=pltpu.VMEM)
    hbm = pl.BlockSpec(memory_space=pl.ANY)
    far = max(chips - 1, 1)
    x_sem = pltpu.SemaphoreType.DMA((2, far, n_chunks))
    y_sem = pltpu.SemaphoreType.DMA((2, far, max(grp_n - 1, 1), n_chunks))
    z_sem = pltpu.SemaphoreType.DMA((2, 2, max(head_n - 1, 1)))
    s_sem = pltpu.SemaphoreType.DMA((1 + chips,))
    return pl.pallas_call(
        functools.partial(gather_kernel, sizes),
        out_shape=(
            jax.ShapeDtypeStruct((out_weight.shape[0], out_weight.shape[1] * ctx_n), dtype),
            jax.ShapeDtypeStruct((steps, resp, width), dtype),
            jax.ShapeDtypeStruct((kinds, steps * resp, cols), dtype),
            jax.ShapeDtypeStruct((2 * heads, DH, DH), jnp.float32),
        ),
        in_specs=[hbm, hbm, vmem, vmem, hbm],
        out_specs=(hbm, vmem, vmem, vmem),
        scratch_shapes=[
            pltpu.VMEM((p_rows + steps * resp, features), dtype),
            pltpu.VMEM((kinds, rows * ctx_n, cols), dtype),
            pltpu.VMEM((steps, resp, features), dtype),
            pltpu.VMEM((2, p_rows, cols), jnp.float32),
            pltpu.VMEM((steps * resp_all, width), jnp.float32),
            pltpu.VMEM((steps, resp_all, width), dtype),
            pltpu.VMEM((2, min(512, embed_table.shape[0] // 4), width), dtype),
            pltpu.SemaphoreType.DMA((2,)),
            pltpu.VMEM((2 * heads, DH, DH), dtype),
            pltpu.VMEM((2 * heads, DH, DH), jnp.float32),
            pltpu.VMEM((heads, DH, DH), dtype),
            pltpu.VMEM((2 * heads, DH, DH), dtype),
            pltpu.VMEM((far, heads, DH, DH), dtype),
            pltpu.VMEM((2, heads, DH, DH), dtype),
            s_sem, s_sem,
            pltpu.VMEM((ctx_n - 1, steps, resp, width), dtype),
            pltpu.VMEM((far, steps, resp, width), dtype),
            pltpu.SemaphoreType.DMA((4,)),
            pltpu.SemaphoreType.DMA((ctx_n - 1,)),
            pltpu.SemaphoreType.DMA((ctx_n - 1,)),
            z_sem, z_sem, x_sem, x_sem, y_sem, y_sem,
            pltpu.SemaphoreType.DMA((2,)), pltpu.SemaphoreType.DMA((2,)),
            x_sem, x_sem, y_sem, y_sem,
        ],
        compiler_params=pltpu.CompilerParams(
            collective_id=0, has_side_effects=True, vmem_limit_bytes=62 * 1024 * 1024
        ),
    )(prompt_hidden, qkv_weight, out_weight, response_ids.reshape(-1, 1), embed_table)


def finish_kernel(head_n, h_ref, of_ref, em_ref, out_ref, weights, w_sem, fresh, mixed, sums, parts,
                  squares, far_squares, t_send, t_recv, q_send, q_recv):
    head = lax.axis_index("head")
    rows, width = em_ref.shape
    have = (head > 0, head + 1 < head_n)

    def weight_copy(to):
        start = pl.multiple_of(to * width, width)
        return pltpu.make_async_copy(of_ref.at[:, pl.ds(start, width)], weights.at[to], w_sem.at[to])

    def product(to):
        weight_copy(to).wait()
        return jnp.dot(h_ref[...], weights[to], preferred_element_type=jnp.float32)

    def term_copy(way, to):
        return remote(sums.at[way, to], parts.at[way, to], t_send.at[way, to], t_recv.at[way, to],
                      {"head": head + (1 if way == 0 else -1)})

    def square_copy(step):
        to = lax.rem(head + step, head_n)
        return remote(squares, far_squares.at[step - 1],
                      q_send.at[step - 1], q_recv.at[step - 1], {"head": to})

    order = []
    for step in range(head_n - 1):
        order += [(0, head_n - 1 - step), (1, step)]

    def ahead(way, to):
        return to > head if way == 0 else to < head

    for way, to in order:
        pl.when(ahead(way, to))(weight_copy(to).start)
    weight_copy(head).start()
    greet((("head", head_n),))
    for way, to in order:
        @pl.when(ahead(way, to))
        def _():
            fresh[...] = product(to)

            @pl.when(have[way])
            def _():
                term_copy(way, to).wait_recv()
                fresh[...] += parts[way, to].astype(jnp.float32)

            sums[way, to] = fresh[...].astype(sums.dtype)
            term_copy(way, to).start()

    mixed[...] = em_ref[...].astype(jnp.float32) + product(head)
    for way in range(2):
        @pl.when(have[way])
        def _():
            term_copy(way, head).wait_recv()
            mixed[...] += parts[way, head].astype(jnp.float32)

    values = mixed[...]
    total = jnp.sum(values * values, axis=-1, keepdims=True)
    total = jnp.broadcast_to(total, (rows, 128)).T[:8]
    squares[...] = total
    for step in range(1, head_n):
        square_copy(step).start()
    for step in range(1, head_n):
        square_copy(step).wait_recv()
        total += far_squares[step - 1]
    total = jnp.broadcast_to(total[:1], (128, rows)).T[:, :1]
    out_ref[...] = (values * lax.rsqrt(total / (width * head_n) + 1e-06)).astype(out_ref.dtype)
    for way, to in order:
        pl.when(ahead(way, to))(term_copy(way, to).wait_send)
    for step in range(1, head_n):
        square_copy(step).wait_send()


def finish(head_n, head_out, full_out, embedded_mine):
    rows, width = embedded_mine.shape
    vmem = pl.BlockSpec(memory_space=pltpu.VMEM)
    others = max(head_n - 1, 1)
    sem = pltpu.SemaphoreType.DMA((others,))
    t_sem = pltpu.SemaphoreType.DMA((2, head_n))
    return pl.pallas_call(
        functools.partial(finish_kernel, head_n),
        out_shape=jax.ShapeDtypeStruct(embedded_mine.shape, jnp.bfloat16),
        in_specs=[vmem, pl.BlockSpec(memory_space=pl.ANY), vmem],
        out_specs=vmem,
        scratch_shapes=[
            pltpu.VMEM((head_n, full_out.shape[0], width), jnp.bfloat16),
            pltpu.SemaphoreType.DMA((head_n,)),
            pltpu.VMEM((rows, width), jnp.float32),
            pltpu.VMEM((rows, width), jnp.float32),
            pltpu.VMEM((2, head_n, rows, width), jnp.bfloat16),
            pltpu.VMEM((2, head_n, rows, width), jnp.bfloat16),
            pltpu.VMEM((8, rows), jnp.float32),
            pltpu.VMEM((others, 8, rows), jnp.float32),
            t_sem, t_sem, sem, sem,
        ],
        compiler_params=pltpu.CompilerParams(collective_id=1, has_side_effects=True),
    )(head_out, full_out, embedded_mine)


def on_device(sizes, prompt_hidden, qkv_weight, out_weight, embed_table, response_ids, assignment):
    local_cols = prompt_hidden.shape[2]
    prompt_rows = prompt_hidden.shape[1]
    head_size = DH
    local_heads = local_cols // head_size
    steps = response_ids.shape[0]
    resp_local = response_ids.shape[1] // lax.axis_size("ctx")
    ctx_index = lax.axis_index("ctx")
    full_out, embedded_mine, projected_qkv, state = gather_all(
        sizes, prompt_hidden.reshape(2 * prompt_rows, local_cols), qkv_weight, out_weight,
        response_ids, embed_table,
    )
    state = state.reshape(2, local_heads, head_size, head_size)
    projected_qkv = projected_qkv.reshape(3, steps, resp_local, local_heads, head_size)
    query = projected_qkv[0]
    key = projected_qkv[1]
    value = projected_qkv[2]
    my_prompt = lax.dynamic_slice_in_dim(assignment, ctx_index * resp_local, resp_local, 0)
    query_f = query.astype(jnp.float32)
    both = jnp.einsum("trhd,phde->ptrhe", query_f, state, precision=lax.Precision.HIGHEST)
    chosen = jnp.where((my_prompt == 0)[None, :, None, None], both[0], both[1])
    scores = jnp.einsum("trhd,srhd->rhts", query, key, preferred_element_type=jnp.float32)
    later = jnp.arange(steps)[:, None] >= jnp.arange(steps)[None, :]
    scores = jnp.where(later[None, None], scores, 0.0).astype(jnp.bfloat16)
    local = jnp.einsum("rhts,srhd->trhd", scores, value, preferred_element_type=jnp.float32)
    head_out = rms_rows(chosen + local).astype(jnp.bfloat16).reshape(steps * resp_local, local_cols)
    result = finish(
        sizes[2], head_out, full_out, embedded_mine.reshape(steps * resp_local, local_cols)
    )
    return result.reshape(steps, resp_local, local_cols)


def solution(mesh):
    sizes = (mesh.shape["grp"], mesh.shape["ctx"], mesh.shape["head"])
    return jax.shard_map(
        functools.partial(on_device, sizes),
        mesh=mesh,
        in_specs=(
            P("grp", "ctx", "head"),
            P(None, "ctx", "head"),
            P("head", "ctx"),
            P("ctx", "head"),
            P(None, "grp"),
            P("grp"),
        ),
        out_specs=P(None, ("grp", "ctx"), "head"),
        check_vma=False,
    )
```

```python
import functools

import jax
import jax.numpy as jnp
from jax import lax
from jax.experimental import pallas as pl
from jax.experimental.pallas import tpu as pltpu
from jax.sharding import PartitionSpec as P

DH = 128
SUB = 4
MESH = pl.DeviceIdType.MESH


def rms_rows(values):
    return values * lax.rsqrt(jnp.mean(values * values, axis=-1, keepdims=True) + 1e-06)


def remote(src, dst, send, recv, target):
    return pltpu.make_async_remote_copy(
        src_ref=src, dst_ref=dst, send_sem=send, recv_sem=recv,
        device_id=target, device_id_type=MESH,
    )


def greet(axes):
    barrier = pltpu.get_barrier_semaphore()
    total = 0
    for axis, size in axes:
        me = lax.axis_index(axis)
        for step in range(1, size):
            pl.semaphore_signal(
                barrier, inc=1, device_id={axis: lax.rem(me + step, size)}, device_id_type=MESH
            )
        total += size - 1
    pl.semaphore_wait(barrier, total)


def gather_kernel(sizes, p_ref, w_ref, o_ref, ids_ref, table_ref, of_ref, em_ref, qkv_ref, state_ref,
                  xa, wf_ref, ef_ref, acc, found, looked_ref, t_tile, t_sem, s_mine, s_chip, s_half, s_mate, s_far, s_back,
                  s_send, s_recv, e_in, e_out, own_sem, e_send, e_recv, z_send, z_recv, x_send, x_recv,
                  y_send, y_recv, pown_send, pown_recv, px_send, px_recv, py_send, py_recv):
    grp_n, ctx_n, head_n = sizes
    chips = ctx_n // 2
    grp, ctx, head = lax.axis_index("grp"), lax.axis_index("ctx"), lax.axis_index("head")
    chip, core = ctx // 2, lax.rem(ctx, 2)
    partner = {"ctx": chip * 2 + 1 - core}
    kinds, rows, cols = w_ref.shape
    o_rows, o_cols = o_ref.shape
    p_rows, width = p_ref.shape
    steps, resp = em_ref.shape[:2]
    r_rows = steps * resp
    heads = cols // DH
    tile = min(256, cols)
    tiles = cols // tile
    w_sub = rows // (grp_n * SUB)
    o_sub = o_rows // (grp_n * SUB)
    chunks = [(kind, sub) for kind in (1, 2, 0, 3) for sub in range(SUB)]

    def chunk_dst(index, shard, part):
        kind, sub = chunks[index]
        if kind == 3:
            start = pl.multiple_of((part * SUB + sub) * o_sub, o_sub)
            return of_ref.at[pl.ds(start, o_sub), pl.ds(pl.multiple_of(shard * o_cols, o_cols), o_cols)]
        start = pl.multiple_of(shard * rows + (part * SUB + sub) * w_sub, w_sub)
        return wf_ref.at[kind, pl.ds(start, w_sub), :]

    def chunk_src(index, part):
        kind, sub = chunks[index]
        if kind == 3:
            return o_ref.at[pl.ds(pl.multiple_of((part * SUB + sub) * o_sub, o_sub), o_sub), :]
        return w_ref.at[kind, pl.ds(pl.multiple_of((part * SUB + sub) * w_sub, w_sub), w_sub), :]

    def prompt_at(owner):
        return xa.at[pl.ds(0, p_rows), pl.ds(pl.multiple_of(owner * width, width), width)]

    def embed_at(owner):
        return ef_ref.at[:, :, pl.ds(pl.multiple_of(owner * width, width), width)]

    def w_at(shard):
        return wf_ref.at[:, pl.ds(pl.multiple_of(shard * rows, rows), rows), :]

    def o_at(shard):
        return of_ref.at[:, pl.ds(pl.multiple_of(shard * o_cols, o_cols), o_cols)]

    greet((("grp", grp_n), ("ctx", ctx_n), ("head", head_n)))

    ends = []

    def at_end(ok, fn):
        ends.append((ok, fn))

    def x_copy(src, index, way, dist, shard):
        return remote(src, chunk_dst(index, shard, grp), x_send.at[way, dist - 1, index],
                      x_recv.at[way, dist - 1, index], {"ctx": ctx + (2 if way == 0 else -2)})

    def z_copy(src, dst, what, way, dist):
        return remote(src, dst, z_send.at[what, way, dist - 1], z_recv.at[what, way, dist - 1],
                      {"head": head + (1 if way == 0 else -1)})

    x_next = (chip + 1 < chips, chip > 0)
    z_next = (head + 1 < head_n, head > 0)

    def start_if(ok, copy):
        pl.when(ok)(copy.start)
        at_end(ok, copy.wait_send)

    for way in range(2):
        start_if(z_next[way], z_copy(p_ref, prompt_at(head), 0, way, 1))
    def x_first(index):
        for way in range(2):
            if chips > 1:
                start_if(x_next[way], x_copy(chunk_src(index, grp), index, way, 1, ctx))

    for index in range(SUB):
        x_first(index)

    mate = chip * 2 + 1 - core
    w_ready, x_ready, ef_ready = [], [], []
    for number, (src, dst, ready) in enumerate(((w_ref, w_at, w_ready), (o_ref, o_at, ends))):
        local = pltpu.make_async_copy(src, dst(ctx), own_sem.at[number])
        local.start()
        ready.append((None, local.wait))
        copy = remote(src, dst(ctx), pown_send.at[number], pown_recv.at[number], partner)
        copy.start()
        at_end(None, copy.wait_send)
        ready.append((None, remote(src, dst(mate), pown_send.at[number], pown_recv.at[number], partner).wait_recv))
    local = pltpu.make_async_copy(p_ref, prompt_at(head), own_sem.at[2])
    local.start()
    x_ready.append((None, local.wait))

    def settle(waits):
        for ok, fn in waits:
            if ok is None:
                fn()
            else:
                pl.when(ok)(fn)
        waits.clear()

    events = []

    vocab = table_ref.shape[0]
    t_rows = t_tile.shape[1]
    n_tiles = vocab // t_rows

    def tile_copy(number, slot):
        start = pl.multiple_of(number * t_rows, t_rows)
        return pltpu.make_async_copy(table_ref.at[pl.ds(start, t_rows), :], t_tile.at[slot], t_sem.at[slot])

    def lookup(first, last):
        tile_copy(first, first % 2).start()
        if first == 0:
            found[...] = jnp.zeros_like(found)

        @pl.loop(first, last)
        def _(number):
            slot = lax.rem(number, 2)

            @pl.when(number + 1 < last)
            def _():
                tile_copy(number + 1, lax.rem(number + 1, 2)).start()

            tile_copy(number, slot).wait()
            names = lax.broadcasted_iota(jnp.int32, (ids_ref.shape[0], t_rows), 1)
            hits = ids_ref[...] == names + (ctx * vocab + number * t_rows)
            pick = jnp.where(hits, 1.0, 0.0).astype(looked_ref.dtype)
            found[...] += jnp.dot(pick, t_tile[slot], preferred_element_type=jnp.float32)

    def embed_send():
        looked_ref[...] = found[...].astype(looked_ref.dtype).reshape(looked_ref.shape)
        for to in range(chips):
            copy = near_copy(to)
            copy.start()
            at_end(None, copy.wait_send)

    def resp_at(owner):
        return pl.ds(pl.multiple_of(owner * resp, resp), resp)

    def near_copy(to):
        return remote(looked_ref.at[:, resp_at(to * 2 + 1 - core), :], e_in.at[to],
                      e_send.at[to], e_recv.at[to], partner)

    def far_rows(step):
        to = lax.rem(chip + step, chips)
        return remote(e_out.at[step - 1], e_in.at[chips + step - 1], e_send.at[chips + step - 1],
                      e_recv.at[chips + step - 1], {"ctx": to * 2 + core})

    def near_sum(to):
        near_copy(to).wait_recv()
        return looked_ref[:, resp_at(to * 2 + core), :].astype(jnp.float32) + e_in[to].astype(jnp.float32)

    def embed_mid():
        for step in range(1, chips):
            e_out[step - 1] = near_sum(lax.rem(chip + step, chips)).astype(e_out.dtype)
            copy = far_rows(step)
            copy.start()
            at_end(None, copy.wait_send)
        for index in range(SUB, 2 * SUB - 1):
            x_first(index)

    def embed_sum():
        total = near_sum(chip)
        for step in range(1, chips):
            far_rows(step).wait_recv()
            total += e_in[chips + step - 1].astype(jnp.float32)
        em_ref[...] = total.astype(em_ref.dtype)
        local = pltpu.make_async_copy(em_ref, embed_at(head), own_sem.at[3])
        local.start()
        ef_ready.append((None, local.wait))
        for way in range(2):
            start_if(z_next[way], z_copy(em_ref, embed_at(head), 1, way, 1))

    def z_event(what, way, dist):
        owner = head - dist if way == 0 else head + dist
        have = owner >= 0 if way == 0 else owner < head_n
        place = (prompt_at, embed_at)[what](owner)

        @pl.when(have)
        def _():
            z_copy(place, place, what, way, dist).wait_recv()

        if dist + 1 < head_n:
            ok = have & z_next[way]
            start_if(ok, z_copy(place, place, what, way, dist + 1))

    for dist in range(1, head_n):
        for way in range(2):
            events.append((22.0 * dist, functools.partial(z_event, 0, way, dist)))
            events.append((22.0 * dist + 14.0, functools.partial(z_event, 1, way, dist)))

    def pass_on(ok, dst, send, recv):
        copy = remote(dst, dst, send, recv, partner)
        start_if(ok, copy)

    mate_ready = {kind: [] for kind in range(4)}

    def mate_wait(index, ok, dst, send, recv):
        mate_ready[chunks[index][0]].append((ok, remote(dst, dst, send, recv, partner).wait_recv))

    def x_event(index, way, dist):
        from_chip = chip - dist if way == 0 else chip + dist
        have = from_chip >= 0 if way == 0 else from_chip < chips
        place = chunk_dst(index, from_chip * 2 + core, grp)
        if way == 0 and dist == 1 and SUB - 1 <= index < len(chunks) - SUB:
            x_first(index + SUB)

        @pl.when(have)
        def _():
            x_copy(place, index, way, dist, from_chip * 2 + core).wait_recv()

        if dist + 1 < chips:
            start_if(have & x_next[way], x_copy(place, index, way, dist + 1, from_chip * 2 + core))
        for step in range(1, grp_n):
            start_if(have, remote(place, place, y_send.at[way, dist - 1, step - 1, index],
                                  y_recv.at[way, dist - 1, step - 1, index],
                                  {"grp": lax.rem(grp + step, grp_n)}))
        sems = px_send.at[way, dist - 1, index], px_recv.at[way, dist - 1, index]
        pass_on(have, place, *sems)
        mate_wait(index, have, chunk_dst(index, from_chip * 2 + 1 - core, grp), *sems)

    def y_event(index, way, dist, step):
        from_chip = chip - dist if way == 0 else chip + dist
        have = from_chip >= 0 if way == 0 else from_chip < chips
        part = lax.rem(grp + grp_n - step, grp_n)
        place = chunk_dst(index, from_chip * 2 + core, part)
        key = (way, dist - 1, step - 1, index)

        @pl.when(have)
        def _():
            remote(place, place, y_send.at[key], y_recv.at[key], partner).wait_recv()

        sems = py_send.at[key], py_recv.at[key]
        pass_on(have, place, *sems)
        mate_wait(index, have, chunk_dst(index, from_chip * 2 + 1 - core, part), *sems)

    def norm_rows():
        settle(ef_ready)
        values = ef_ref[...].astype(jnp.float32).reshape(r_rows, ef_ref.shape[2])
        xa[pl.ds(p_rows, r_rows), :] = rms_rows(values).astype(xa.dtype)

    def lanes_of(number):
        return pl.ds(pl.multiple_of(number * tile, tile), tile)

    def prompt_dots(dist):
        settle(x_ready)
        settle(w_ready)
        settle(mate_ready[1])
        settle(mate_ready[2])
        for way in range(2 if dist else 1):
            owner = head - dist if way == 0 else head + dist
            have = owner >= 0 if way == 0 else owner < head_n
            block = pl.ds(pl.multiple_of(owner * width, width), width)

            @pl.when(have)
            def _():
                @pl.loop(0, 2 * tiles)
                def _(number):
                    kind = number // tiles
                    lanes = lanes_of(lax.rem(number, tiles))
                    out = jnp.dot(xa[pl.ds(0, p_rows), block], wf_ref[1 + kind, block, lanes],
                                  preferred_element_type=jnp.float32)
                    if dist:
                        acc[kind, :, lanes] += out
                    else:
                        acc[kind, :, lanes] = out

    def project(kind):
        settle(mate_ready[kind])

        @pl.loop(0, tiles)
        def _(number):
            lanes = lanes_of(number)
            out = jnp.dot(xa[pl.ds(p_rows, r_rows), :], wf_ref[kind, :, lanes],
                          preferred_element_type=jnp.float32)
            qkv_ref[kind, :, lanes] = out.astype(qkv_ref.dtype)

    def to_mate(src, dst, number):
        return remote(src, dst, s_send.at[number], s_recv.at[number], partner)

    def make_state():
        span = p_rows // 2

        @pl.loop(0, 2 * heads)
        def _(number):
            rows_at = pl.ds(pl.multiple_of(number // heads * span, span), span)
            lanes = pl.ds(pl.multiple_of(lax.rem(number, heads) * DH, DH), DH)
            s_chip[number] = lax.dot_general(
                acc[0, rows_at, lanes].astype(s_mine.dtype), acc[1, rows_at, lanes].astype(s_mine.dtype), (((0,), (0,)), ((), ())),
                preferred_element_type=jnp.float32,
            )
        s_mine[...] = s_chip[...].astype(s_mine.dtype)
        copy = to_mate(s_mine, s_mate, 0)
        copy.start()
        at_end(None, copy.wait_send)

    mine = pl.ds(core * heads, heads)
    theirs = pl.ds((1 - core) * heads, heads)

    def far_copy(step):
        other = lax.rem(chip + step, chips)
        return remote(s_half, s_far.at[step - 1], s_send.at[1 + step], s_recv.at[1 + step],
                      {"ctx": other * 2 + core})

    def chip_state():
        to_mate(s_mine, s_mate, 0).wait_recv()
        s_chip[...] = s_chip[...] + s_mate[...].astype(jnp.float32)
        s_half[...] = s_chip[mine].astype(s_half.dtype)
        for step in range(1, chips):
            copy = far_copy(step)
            copy.start()
            at_end(None, copy.wait_send)

    def whole_state():
        total = s_chip[mine]
        for step in range(1, chips):
            far_copy(step).wait_recv()
            total = total + s_far[step - 1].astype(jnp.float32)
        state_ref[mine] = total
        s_back[0] = total.astype(s_back.dtype)
        copy = to_mate(s_back.at[0], s_back.at[1], 1)
        copy.start()
        at_end(None, copy.wait_send)

    def mate_state():
        to_mate(s_back.at[0], s_back.at[1], 1).wait_recv()
        state_ref[theirs] = s_back[1].astype(jnp.float32)

    unit = 22.0 / SUB

    def reach(chunk):
        return unit * (chunk + 2) + 88.0 * max(chips - 2, 0) + 1.5

    for part in range(4):
        events.append((unit * part + 0.1 if part else 0.0,
                       functools.partial(lookup, n_tiles * part // 4, n_tiles * (part + 1) // 4)))
    events.append((unit * 3 + 0.2, embed_send))
    events.append((unit * 3 + 0.3, embed_mid))
    events.append((30.0, embed_sum))
    for dist in range(1, chips):
        for index in range(len(chunks)):
            when = unit * (index + 1) + 88.0 * (dist - 1)
            for way in range(2):
                events.append((when, functools.partial(x_event, index, way, dist)))
                for step in range(1, grp_n):
                    events.append((when + unit + 1.0, functools.partial(y_event, index, way, dist, step)))
    ready = reach(2 * SUB - 1)
    after = ready
    for dist in range(head_n):
        after = max(ready + 0.1 * dist, 22.0 * dist + 0.5)
        events.append((after, functools.partial(prompt_dots, dist)))
    embedded_at = 22.0 * (head_n - 1) + 20.5
    events.append((after + 0.1, make_state))
    events.append((after + 0.2, chip_state))
    embedded_at -= 6.0
    after = max(after + 0.3, embedded_at)
    events.append((after, norm_rows))
    events.append((after + 0.2, functools.partial(project, 1)))
    events.append((after + 3.0, functools.partial(project, 2)))
    events.append((max(after + 6.0, reach(3 * SUB - 1)), functools.partial(project, 0)))
    events.append((max(after + 12.0, reach(4 * SUB - 1) - 6.0), whole_state))
    last = max(when for when, _ in events)
    events.append((last + 50.0, mate_state))
    for _, fn in sorted(events, key=lambda event: event[0]):
        fn()
    settle(mate_ready[3])
    settle(ends)


def gather_all(sizes, prompt_hidden, qkv_weight, out_weight, response_ids, embed_table):
    grp_n, ctx_n, head_n = sizes
    chips = ctx_n // 2
    kinds, rows, cols = qkv_weight.shape
    steps, resp_all = response_ids.shape
    width = prompt_hidden.shape[1]
    resp = resp_all // ctx_n
    p_rows = prompt_hidden.shape[0]
    heads = cols // DH
    features = width * head_n
    n_chunks = (kinds + 1) * SUB
    dtype = prompt_hidden.dtype
    vmem = pl.BlockSpec(memory_space=pltpu.VMEM)
    hbm = pl.BlockSpec(memory_space=pl.ANY)
    far = max(chips - 1, 1)
    x_sem = pltpu.SemaphoreType.DMA((2, far, n_chunks))
    y_sem = pltpu.SemaphoreType.DMA((2, far, max(grp_n - 1, 1), n_chunks))
    z_sem = pltpu.SemaphoreType.DMA((2, 2, max(head_n - 1, 1)))
    s_sem = pltpu.SemaphoreType.DMA((1 + chips,))
    return pl.pallas_call(
        functools.partial(gather_kernel, sizes),
        out_shape=(
            jax.ShapeDtypeStruct((out_weight.shape[0], out_weight.shape[1] * ctx_n), dtype),
            jax.ShapeDtypeStruct((steps, resp, width), dtype),
            jax.ShapeDtypeStruct((kinds, steps * resp, cols), dtype),
            jax.ShapeDtypeStruct((2 * heads, DH, DH), jnp.float32),
        ),
        in_specs=[hbm, hbm, vmem, vmem, hbm],
        out_specs=(hbm, vmem, vmem, vmem),
        scratch_shapes=[
            pltpu.VMEM((p_rows + steps * resp, features), dtype),
            pltpu.VMEM((kinds, rows * ctx_n, cols), dtype),
            pltpu.VMEM((steps, resp, features), dtype),
            pltpu.VMEM((2, p_rows, cols), jnp.float32),
            pltpu.VMEM((steps * resp_all, width), jnp.float32),
            pltpu.VMEM((steps, resp_all, width), dtype),
            pltpu.VMEM((2, min(512, embed_table.shape[0] // 4), width), dtype),
            pltpu.SemaphoreType.DMA((2,)),
            pltpu.VMEM((2 * heads, DH, DH), dtype),
            pltpu.VMEM((2 * heads, DH, DH), jnp.float32),
            pltpu.VMEM((heads, DH, DH), dtype),
            pltpu.VMEM((2 * heads, DH, DH), dtype),
            pltpu.VMEM((far, heads, DH, DH), dtype),
            pltpu.VMEM((2, heads, DH, DH), dtype),
            s_sem, s_sem,
            pltpu.VMEM((ctx_n - 1, steps, resp, width), dtype),
            pltpu.VMEM((far, steps, resp, width), dtype),
            pltpu.SemaphoreType.DMA((4,)),
            pltpu.SemaphoreType.DMA((ctx_n - 1,)),
            pltpu.SemaphoreType.DMA((ctx_n - 1,)),
            z_sem, z_sem, x_sem, x_sem, y_sem, y_sem,
            pltpu.SemaphoreType.DMA((2,)), pltpu.SemaphoreType.DMA((2,)),
            x_sem, x_sem, y_sem, y_sem,
        ],
        compiler_params=pltpu.CompilerParams(
            collective_id=0, has_side_effects=True, vmem_limit_bytes=62 * 1024 * 1024
        ),
    )(prompt_hidden, qkv_weight, out_weight, response_ids.reshape(-1, 1), embed_table)


def finish_kernel(head_n, h_ref, of_ref, em_ref, out_ref, weights, w_sem, fresh, mixed, sums, parts,
                  squares, far_squares, t_send, t_recv, q_send, q_recv):
    head = lax.axis_index("head")
    rows, width = em_ref.shape
    have = (head > 0, head + 1 < head_n)

    def weight_copy(to):
        start = pl.multiple_of(to * width, width)
        return pltpu.make_async_copy(of_ref.at[:, pl.ds(start, width)], weights.at[to], w_sem.at[to])

    def product(to):
        weight_copy(to).wait()
        return jnp.dot(h_ref[...], weights[to], preferred_element_type=jnp.float32)

    def term_copy(way, to):
        return remote(sums.at[way, to], parts.at[way, to], t_send.at[way, to], t_recv.at[way, to],
                      {"head": head + (1 if way == 0 else -1)})

    def square_copy(step):
        to = lax.rem(head + step, head_n)
        return remote(squares, far_squares.at[step - 1],
                      q_send.at[step - 1], q_recv.at[step - 1], {"head": to})

    order = []
    for step in range(head_n - 1):
        order += [(0, head_n - 1 - step), (1, step)]

    def ahead(way, to):
        return to > head if way == 0 else to < head

    for way, to in order:
        pl.when(ahead(way, to))(weight_copy(to).start)
    weight_copy(head).start()
    greet((("head", head_n),))
    for way, to in order:
        @pl.when(ahead(way, to))
        def _():
            fresh[...] = product(to)

            @pl.when(have[way])
            def _():
                term_copy(way, to).wait_recv()
                fresh[...] += parts[way, to].astype(jnp.float32)

            sums[way, to] = fresh[...].astype(sums.dtype)
            term_copy(way, to).start()

    mixed[...] = em_ref[...].astype(jnp.float32) + product(head)
    for way in range(2):
        @pl.when(have[way])
        def _():
            term_copy(way, head).wait_recv()
            mixed[...] += parts[way, head].astype(jnp.float32)

    values = mixed[...]
    total = jnp.sum(values * values, axis=-1, keepdims=True)
    total = jnp.broadcast_to(total, (rows, 128)).T[:8]
    squares[...] = total
    for step in range(1, head_n):
        square_copy(step).start()
    for step in range(1, head_n):
        square_copy(step).wait_recv()
        total += far_squares[step - 1]
    total = jnp.broadcast_to(total[:1], (128, rows)).T[:, :1]
    out_ref[...] = (values * lax.rsqrt(total / (width * head_n) + 1e-06)).astype(out_ref.dtype)
    for way, to in order:
        pl.when(ahead(way, to))(term_copy(way, to).wait_send)
    for step in range(1, head_n):
        square_copy(step).wait_send()


def finish(head_n, head_out, full_out, embedded_mine):
    rows, width = embedded_mine.shape
    vmem = pl.BlockSpec(memory_space=pltpu.VMEM)
    others = max(head_n - 1, 1)
    sem = pltpu.SemaphoreType.DMA((others,))
    t_sem = pltpu.SemaphoreType.DMA((2, head_n))
    return pl.pallas_call(
        functools.partial(finish_kernel, head_n),
        out_shape=jax.ShapeDtypeStruct(embedded_mine.shape, jnp.bfloat16),
        in_specs=[vmem, pl.BlockSpec(memory_space=pl.ANY), vmem],
        out_specs=vmem,
        scratch_shapes=[
            pltpu.VMEM((head_n, full_out.shape[0], width), jnp.bfloat16),
            pltpu.SemaphoreType.DMA((head_n,)),
            pltpu.VMEM((rows, width), jnp.float32),
            pltpu.VMEM((rows, width), jnp.float32),
            pltpu.VMEM((2, head_n, rows, width), jnp.bfloat16),
            pltpu.VMEM((2, head_n, rows, width), jnp.bfloat16),
            pltpu.VMEM((8, rows), jnp.float32),
            pltpu.VMEM((others, 8, rows), jnp.float32),
            t_sem, t_sem, sem, sem,
        ],
        compiler_params=pltpu.CompilerParams(collective_id=1, has_side_effects=True),
    )(head_out, full_out, embedded_mine)


def on_device(sizes, prompt_hidden, qkv_weight, out_weight, embed_table, response_ids, assignment):
    local_cols = prompt_hidden.shape[2]
    prompt_rows = prompt_hidden.shape[1]
    head_size = DH
    local_heads = local_cols // head_size
    steps = response_ids.shape[0]
    resp_local = response_ids.shape[1] // lax.axis_size("ctx")
    ctx_index = lax.axis_index("ctx")
    full_out, embedded_mine, projected_qkv, state = gather_all(
        sizes, prompt_hidden.reshape(2 * prompt_rows, local_cols), qkv_weight, out_weight,
        response_ids, embed_table,
    )
    state = state.reshape(2, local_heads, head_size, head_size)
    projected_qkv = projected_qkv.reshape(3, steps, resp_local, local_heads, head_size)
    query = projected_qkv[0]
    key = projected_qkv[1]
    value = projected_qkv[2]
    my_prompt = lax.dynamic_slice_in_dim(assignment, ctx_index * resp_local, resp_local, 0)
    query_f = query.astype(jnp.float32)
    both = jnp.einsum("trhd,phde->ptrhe", query_f, state, precision=lax.Precision.HIGHEST)
    chosen = jnp.where((my_prompt == 0)[None, :, None, None], both[0], both[1])
    scores = jnp.einsum("trhd,srhd->rhts", query, key, preferred_element_type=jnp.float32)
    later = jnp.arange(steps)[:, None] >= jnp.arange(steps)[None, :]
    scores = jnp.where(later[None, None], scores, 0.0).astype(jnp.bfloat16)
    local = jnp.einsum("rhts,srhd->trhd", scores, value, preferred_element_type=jnp.float32)
    head_out = rms_rows(chosen + local).astype(jnp.bfloat16).reshape(steps * resp_local, local_cols)
    result = finish(
        sizes[2], head_out, full_out, embedded_mine.reshape(steps * resp_local, local_cols)
    )
    return result.reshape(steps, resp_local, local_cols)


def solution(mesh):
    sizes = (mesh.shape["grp"], mesh.shape["ctx"], mesh.shape["head"])
    return jax.shard_map(
        functools.partial(on_device, sizes),
        mesh=mesh,
        in_specs=(
            P("grp", "ctx", "head"),
            P(None, "ctx", "head"),
            P("head", "ctx"),
            P("ctx", "head"),
            P(None, "grp"),
            P("grp"),
        ),
        out_specs=P(None, ("grp", "ctx"), "head"),
        check_vma=False,
    )
```
